32 devices in a mesh: ctx: 4 (over y, x), ep: 8 (over z, core).
Axes of the slice: x: 2, y: 2, z: 4, core: 2. Of those that a mesh axis runs over, the one named last changes fastest.
Arguments:
- block_input: bfloat16 [8, 512, 768], P('ep', 'ctx'), may hold values from -36 to 36
- out_grad: bfloat16 [8, 512, 768], P('ep', 'ctx'), may hold values from -6 to 6
- w_query: bfloat16 [768, 768], P('ep'), may hold values from -0.21875 to 0.21875
- w_key: bfloat16 [768, 768], P('ep'), may hold values from -0.21875 to 0.21875
- w_value: bfloat16 [768, 768], P('ep'), may hold values from -0.21875 to 0.21875
- w_output: bfloat16 [768, 768], P('ep'), may hold values from -0.875 to 0.875
- w_router: bfloat16 [768, 64], P('ep'), may hold values from -0.4375 to 0.4375
- attn_gain: bfloat16 [768], P('ep'), may hold values from 0.25 to 1.75
- moe_gain: bfloat16 [768], P('ep'), may hold values from 0.25 to 1.75
- bias_table: bfloat16 [32, 12], P('ep'), may hold values from -6 to 303
- rel_bucket: int32 [512], replicated, may hold values from 0 to 31
- expert_ids: int32 [8, 512, 2], P('ep', 'ctx'), may hold values from 0 to 63, all different within a row; in each aligned block of 128 rows (0 to 127, 128 to 255, ..., all dimensions but the last counted through in order) at most 6 rows name the same one
- expert_in: bfloat16 [64, 768, 3072], P('ep', None, 'ctx'), may hold values from -0.21875 to 0.21875
- expert_out: bfloat16 [64, 3072, 768], P('ep', 'ctx'), may hold values from -0.109375 to 0.109375
Outputs:
- block_output: float32 [8, 512, 768], P('ep', 'ctx')
- input_grad: float32 [8, 512, 768], P('ep', 'ctx')
- grad_query: float32 [768, 768], P('ep')
- grad_key: float32 [768, 768], P('ep')
- grad_value: float32 [768, 768], P('ep')
- grad_output: float32 [768, 768], P('ep')
- grad_router: float32 [768, 64], P('ep')
- grad_attn_gain: float32 [768], P('ep')
- grad_moe_gain: float32 [768], P('ep')
- grad_bias_table: float32 [32, 12], P('ep')
- grad_expert_in: float32 [64, 768, 3072], P('ep', None, 'ctx')
- grad_expert_out: float32 [64, 3072, 768], P('ep', 'ctx')
The draws below stay inside these ranges and needn't reach their ends.
Inputs may be any that keep to these rules, and one draw needn't show every extreme that they name: `expert_ids`: each token names two different experts. Within each block of 128 positions of a sequence starting at a multiple of 128, no expert is named by more than 6 tokens, and some block has an expert named by exactly 6.
All inputs are finite; a program needn't handle non-finite values.
Results may differ from the reference program's by a relative error of at most 0.014.
Values may be sent and summed in bfloat16 or wider, within the bound.
No kernel may reach another device: no remote copies, remote signals or barrier semaphores. Data moves between devices by JAX's collectives and lax.ppermute only.
A program may use at most 448 MiB of HBM per device.

```python
import math
import jax
import jax.numpy as jnp
import numpy as np
from jax import lax

D = 768
H = 12
HD = 64
FF = 3072
E = 64
NB = 32
BLK = 128
CAP = 6
LEN = 512
SEQS = 8


def draw_block_input(key, part):
    key_rows, key_cols, key_base = jax.random.split(key, 3)
    row_scale = jnp.exp(jax.random.uniform(key_rows, (SEQS, LEN, 1), jnp.float32, math.log(0.3), math.log(3.0)))
    col_scale = jnp.exp(jax.random.uniform(key_cols, (1, 1, D), jnp.float32, math.log(0.3), math.log(3.0)))
    base_vals = jax.random.truncated_normal(key_base, -4.0, 4.0, (SEQS, LEN, D), jnp.float32)
    return (base_vals * row_scale * col_scale).astype(jnp.bfloat16)


def draw_bias_table(key, part):
    key_base = jax.random.fold_in(key, 0)
    base_vals = jax.random.truncated_normal(key_base, -4.0, 4.0, (NB, H), jnp.float32) * 1.5
    table_vals = base_vals
    return table_vals.astype(jnp.bfloat16)


def touch_ends(entries, rng, least, high):
    spot = [jax.random.randint(jax.random.fold_in(rng, axis), (), 0, length) for axis, length in enumerate(entries.shape)]
    main_axis = entries.shape.index(max(entries.shape))
    neighbour = spot[:main_axis] + [(spot[main_axis] + 1) % entries.shape[main_axis]] + spot[main_axis + 1:]
    return entries.at[tuple(spot)].set(least).at[tuple(neighbour)].set(high)


def shard_levels(rng, dims, shards, smallest, largest):
    def one(axis_at, parts):
        heights = jax.random.uniform(jax.random.fold_in(jax.random.fold_in(rng, 6), axis_at), (parts,), jnp.float32, smallest / len(shards), largest / len(shards))
        return jnp.repeat(jnp.exp(heights), dims[axis_at] // parts).reshape((-1,) + (1,) * (len(dims) - axis_at - 1))

    factor_of = one(*shards[0])
    for cut in shards[1:]:
        factor_of = factor_of * one(*cut)
    return factor_of


def assign_block(key, own, number, rows, amount, top, reach, slope):
    ranking = jax.random.permutation(key, amount)
    heavy_load, usual = load_shares(amount, rows * top, reach, slope, True), load_shares(amount, rows * top, reach, slope, False)
    places = jnp.arange(amount)

    def named(lengths, offset_by):
        used = int((lengths > 0).sum())
        fixed = max(1, used // 4)
        passed = fixed + (places - fixed + offset_by * (used - fixed)) % max(1, amount - fixed)
        return jnp.zeros((amount,), jnp.int32).at[ranking[jnp.where(places < fixed, places, passed)]].set(jnp.asarray(lengths, jnp.int32))

    lengths = jnp.where(number % 4 == 0, named(heavy_load, number // 4), named(usual, number - number // 4 - 1))
    mixed = jax.random.permutation(jax.random.fold_in(own, 3), amount)
    donor, taker = mixed[0:amount // 2 * 2:2], mixed[1:amount // 2 * 2:2]
    slack = jnp.minimum(lengths[donor] - 1, reach - lengths[taker]) // 2
    slack = jnp.where((donor == ranking[0]) | (taker == ranking[0]) | (lengths[taker] == 0), 0, jnp.maximum(slack, 0))
    passed = jax.random.randint(jax.random.fold_in(own, 4), (amount // 2,), 0, 1 << 20) % (slack + 1)
    lengths = lengths.at[donor].add(-passed).at[taker].add(passed)
    items = jnp.searchsorted(jnp.cumsum(lengths), jnp.arange(rows * top), side="right").astype(jnp.int32)
    listing = items.reshape(top, rows).T
    listing = listing[jax.random.permutation(jax.random.fold_in(own, 1), rows)]
    offset_by = jax.random.randint(jax.random.fold_in(own, 2), (rows, 1), 0, top)
    return jnp.take_along_axis(listing, (jnp.arange(top)[None, :] + offset_by) % top, axis=1)


def load_shares(amount, total, limit, lean, full):
    loads = [(1 << 20) // math.isqrt(rank ** lean) + 1 for rank in range(1, amount + 1)]
    largest = limit if full else min(limit, max(-(-total // amount), total * loads[0] // sum(loads)))
    least = 1 if total - largest >= amount - 1 else 0
    holding, surplus = [largest] + [least] * (amount - 1), total - largest - least * (amount - 1)
    while surplus > 0:
        candidates = [i for i in range(1, amount) if holding[i] < largest] or [i for i in range(1, amount) if holding[i] < limit]
        mass, budget = sum([loads[i] for i in candidates]), surplus
        for i in candidates:
            addition = min(limit - holding[i], max(1, budget * loads[i] // mass), surplus)
            holding[i] = holding[i] + addition
            surplus = surplus - addition
    return np.array(holding)


def normal_values(own_key, dims, scale, bound, shards=(), dtype=jnp.bfloat16):
    values = jax.random.normal(own_key, dims, jnp.float32) * scale
    if len(shards) > 0:
        values = shard_levels(own_key, dims, shards, -0.22, 0.18) * values
    return jnp.clip(values, min=-bound, max=bound).astype(dtype)


def setup_inputs(seed: int = 0) -> dict:
    seeds = jax.random.split(jax.random.key(seed), 15)
    block_input = draw_block_input(jax.random.fold_in(seeds[14], 71), 0)
    out_grad = normal_values(seeds[1], (SEQS, LEN, D), 1.0, 6.0, ((0, 8), (1, 4)))
    w_query = normal_values(seeds[2], (D, D), D ** -0.5, 0.21875, ((0, 8),))
    w_key = normal_values(seeds[3], (D, D), D ** -0.5, 0.21875, ((0, 8),))
    w_value = normal_values(seeds[4], (D, D), D ** -0.5, 0.21875, ((0, 8),))
    w_output = normal_values(seeds[5], (D, D), (D // 16) ** -0.5, 0.875, ((0, 8),))
    w_router = normal_values(seeds[6], (D, E), (D // 4) ** -0.5, 0.4375, ((0, 8),))
    attn_gain = jnp.clip(1.0 + 0.15 * jax.random.normal(seeds[7], (D,), jnp.float32), 0.25, 1.75).astype(jnp.bfloat16)
    moe_gain = jnp.clip(1.0 + 0.15 * jax.random.normal(seeds[8], (D,), jnp.float32), 0.25, 1.75).astype(jnp.bfloat16)
    bias_table = draw_bias_table(jax.random.fold_in(seeds[14], 71), 0)
    rel_bucket = touch_ends(jax.random.randint(seeds[10], (LEN,), 0, NB), jax.random.fold_in(seeds[10], 1), 0, NB - 1).astype(jnp.int32)
    expert_ids_keys = jax.random.split(jax.random.fold_in(seeds[11], 1), SEQS * LEN // BLK)
    expert_ids_turns = jax.random.permutation(jax.random.fold_in(seeds[11], 3), SEQS * LEN // BLK)
    expert_ids = jax.vmap(lambda own, number: assign_block(jax.random.fold_in(seeds[11], 2), own, number, BLK, E, 2, CAP, 1))(expert_ids_keys, expert_ids_turns).reshape((SEQS, LEN, 2))
    expert_in = normal_values(seeds[12], (E, D, FF), D ** -0.5, 0.21875, ((0, 8), (2, 4)))
    expert_out = normal_values(seeds[13], (E, FF, D), FF ** -0.5, 0.109375, ((0, 8), (1, 4)))
    return dict(block_input=block_input, out_grad=out_grad, w_query=w_query, w_key=w_key, w_value=w_value, w_output=w_output, w_router=w_router, attn_gain=attn_gain, moe_gain=moe_gain, bias_table=bias_table, rel_bucket=rel_bucket, expert_ids=expert_ids, expert_in=expert_in, expert_out=expert_out)


EPS = 1e-06
SCALE = 0.125
INV_ROOT_TWO = 1.0 / math.sqrt(2.0)
INV_ROOT_TAU = 1.0 / math.sqrt(2.0 * math.pi)

def as_float(tensor):
    return tensor.astype(jnp.float32)

def as_half(tensor):
    return tensor.astype(jnp.bfloat16)

def round_half(tensor):
    return as_float(lax.optimization_barrier(as_half(tensor)))

def rms_apply(tensor, gain_row):
    inverse = lax.rsqrt(lax.optimization_barrier(jnp.mean(tensor * tensor, axis=-1, keepdims=True)) + EPS)
    unit_vals = tensor * inverse
    return (unit_vals, inverse, unit_vals * gain_row)

def rms_back(upstream, unit_vals, inverse, gain_row):
    scaled = upstream * gain_row
    gain_grad = lax.optimization_barrier(jnp.sum(upstream * unit_vals, axis=0))
    moved_grad = inverse * (scaled - unit_vals * lax.optimization_barrier(jnp.mean(scaled * unit_vals, axis=-1, keepdims=True)))
    return (moved_grad, gain_grad)

def gelu_value(preact):
    return preact * 0.5 * (1.0 + lax.erf(preact * INV_ROOT_TWO))

def gelu_slope(preact):
    return 0.5 * (1.0 + lax.erf(preact * INV_ROOT_TWO)) + preact * jnp.exp(-0.5 * preact * preact) * INV_ROOT_TAU

def seq_offsets():
    positions = jnp.arange(LEN).astype(jnp.int32)
    return positions[:, None] - positions[None, :]

def seq_attention(tokens, params):
    w_query, w_key, w_value, w_output, attn_gain, offset_bias = params
    token_float = as_float(tokens)
    unit_one, inv_one, normed_one = rms_apply(token_float, as_float(attn_gain))
    hidden_one = as_half(normed_one)
    queries = as_half(jnp.dot(hidden_one, w_query, preferred_element_type=jnp.float32) * SCALE)
    key_rows = as_half(jnp.dot(hidden_one, w_key, preferred_element_type=jnp.float32))
    value_rows = as_half(jnp.dot(hidden_one, w_value, preferred_element_type=jnp.float32))
    offsets = seq_offsets()
    bias_full = jnp.take(offset_bias.T, jnp.clip(offsets, 0, LEN - 1), axis=1)
    scores = jnp.einsum('ihd,jhd->hij', as_float(queries).reshape(LEN, H, HD), as_float(key_rows).reshape(LEN, H, HD)) + bias_full
    scores = jnp.where(offsets[None] >= 0, scores, -jnp.inf)
    row_peak = lax.optimization_barrier(jnp.max(scores, axis=-1, keepdims=True))
    logsum = row_peak + jnp.log(lax.optimization_barrier(jnp.sum(jnp.exp(scores - row_peak), axis=-1, keepdims=True)))
    probs = round_half(jnp.exp(scores - logsum))
    attended = as_half(jnp.einsum('hij,jhd->ihd', probs, as_float(value_rows).reshape(LEN, H, HD)).reshape(LEN, D))
    mixed_sum = token_float + jnp.dot(attended, w_output, preferred_element_type=jnp.float32)
    saved_state = (unit_one, inv_one, hidden_one, queries, key_rows, value_rows, scores, logsum, probs, attended, offsets)
    return (mixed_sum, saved_state)

def reference(block_input, out_grad, w_query, w_key, w_value, w_output, w_router, attn_gain, moe_gain, bias_table, rel_bucket, expert_ids, expert_in, expert_out):
    bucket_hot = (rel_bucket[:, None] == jnp.arange(NB).astype(jnp.int32)[None, :]).astype(jnp.float32)
    offset_bias = jnp.dot(bucket_hot, as_float(bias_table), precision=lax.Precision.HIGHEST)
    attn_params = (w_query, w_key, w_value, w_output, attn_gain, offset_bias)
    mixed_all = lax.map(lambda tokens: seq_attention(tokens, attn_params)[0], block_input)
    rows_all = SEQS * LEN
    mixed_flat = mixed_all.reshape(rows_all, D)
    moe_unit, moe_inv, normed_two = rms_apply(mixed_flat, as_float(moe_gain))
    hidden_two = as_half(normed_two)
    logits = jnp.dot(hidden_two, w_router, preferred_element_type=jnp.float32)
    routed = expert_ids.reshape(rows_all, 2).astype(jnp.int32)
    logit_first = jnp.take_along_axis(logits, routed[:, 0:1], axis=1)
    logit_second = jnp.take_along_axis(logits, routed[:, 1:2], axis=1)
    gate_first = jax.nn.sigmoid(logit_first - logit_second)
    gate_second = jax.nn.sigmoid(logit_second - logit_first)
    expert_iota = jnp.arange(E).astype(jnp.int32)
    chosen = (routed[:, 0:1] == expert_iota[None, :]).astype(jnp.int32) + (routed[:, 1:2] == expert_iota[None, :]).astype(jnp.int32)
    block_total = rows_all // BLK
    chosen_blocks = chosen.reshape(block_total, BLK, E)
    earlier_count = (jnp.cumsum(chosen_blocks, axis=1) - chosen_blocks).reshape(rows_all, E).astype(jnp.int32)
    block_index = (jnp.arange(rows_all).astype(jnp.int32) // BLK).astype(jnp.int32)
    slot_first = block_index * CAP + jnp.take_along_axis(earlier_count, routed[:, 0:1], axis=1)[:, 0]
    slot_second = block_index * CAP + jnp.take_along_axis(earlier_count, routed[:, 1:2], axis=1)[:, 0]
    slot_total = block_total * CAP
    expert_rows = jnp.zeros((E, slot_total, D), jnp.bfloat16)
    expert_rows = expert_rows.at[routed[:, 0], slot_first].set(hidden_two).at[routed[:, 1], slot_second].set(hidden_two)

    def expert_forward(operands):
        slot_rows, weight_in, weight_out = operands
        preact = jnp.dot(slot_rows, weight_in, preferred_element_type=jnp.float32)
        active = as_half(gelu_value(preact))
        return as_half(jnp.dot(active, weight_out, preferred_element_type=jnp.float32))
    results = lax.map(expert_forward, (expert_rows, expert_in, expert_out))
    result_first = as_float(results[routed[:, 0], slot_first])
    result_second = as_float(results[routed[:, 1], slot_second])
    block_output = mixed_flat + (gate_first * result_first + gate_second * result_second)
    upstream = as_float(out_grad).reshape(rows_all, D)
    grad_result_first = as_half(gate_first * upstream)
    grad_result_second = as_half(gate_second * upstream)
    grad_slots = jnp.zeros((E, slot_total, D), jnp.bfloat16)
    grad_slots = grad_slots.at[routed[:, 0], slot_first].set(grad_result_first).at[routed[:, 1], slot_second].set(grad_result_second)

    def expert_backward(operands):
        slot_rows, grad_out_rows, weight_in, weight_out = operands
        preact = jnp.dot(slot_rows, weight_in, preferred_element_type=jnp.float32)
        active = as_half(gelu_value(preact))
        grad_active = jnp.dot(grad_out_rows, weight_out.T, preferred_element_type=jnp.float32)
        grad_preact = as_half(grad_active * gelu_slope(preact))
        grad_in = jnp.dot(slot_rows.T, grad_preact, preferred_element_type=jnp.float32)
        grad_out = jnp.dot(active.T, grad_out_rows, preferred_element_type=jnp.float32)
        grad_back = as_half(jnp.dot(grad_preact, weight_in.T, preferred_element_type=jnp.float32))
        return (grad_in, grad_out, grad_back)
    grad_expert_in, grad_expert_out, grad_back = lax.map(expert_backward, (expert_rows, grad_slots, expert_in, expert_out))
    grad_gate_first = lax.optimization_barrier(jnp.sum(upstream * result_first, axis=-1, keepdims=True))
    grad_gate_second = lax.optimization_barrier(jnp.sum(upstream * result_second, axis=-1, keepdims=True))
    grad_logit = gate_first * gate_second * (grad_gate_first - grad_gate_second)
    pick_first = (routed[:, 0:1] == expert_iota[None, :]).astype(jnp.float32)
    pick_second = (routed[:, 1:2] == expert_iota[None, :]).astype(jnp.float32)
    grad_logits = as_half(grad_logit * (pick_first - pick_second))
    grad_router = jnp.dot(hidden_two.T, grad_logits, preferred_element_type=jnp.float32)
    grad_hidden_two = as_float(grad_back[routed[:, 0], slot_first]) + as_float(grad_back[routed[:, 1], slot_second])
    grad_hidden_two = grad_hidden_two + jnp.dot(grad_logits, w_router.T, preferred_element_type=jnp.float32)
    moved_two, grad_moe_gain = rms_back(grad_hidden_two, moe_unit, moe_inv, as_float(moe_gain))
    grad_mixed = (upstream + moved_two).reshape(SEQS, LEN, D)

    def seq_back(totals, inputs):
        tokens, grad_mix = inputs
        mixed_unused, saved_state = seq_attention(tokens, attn_params)
        unit_one, inv_one, hidden_one, queries, key_rows, value_rows, scores, logsum, probs, attended, offsets = saved_state
        grad_mix_half = as_half(grad_mix)
        grad_attended = as_half(jnp.dot(grad_mix_half, w_output.T, preferred_element_type=jnp.float32))
        grad_w_output = jnp.dot(attended.T, grad_mix_half, preferred_element_type=jnp.float32)
        grad_heads = as_float(grad_attended).reshape(LEN, H, HD)
        grad_values_full = jnp.einsum('hij,ihd->jhd', probs, grad_heads).reshape(LEN, D)
        grad_probs = jnp.einsum('ihd,jhd->hij', grad_heads, as_float(value_rows).reshape(LEN, H, HD))
        row_delta = lax.optimization_barrier(jnp.sum(grad_heads * as_float(attended).reshape(LEN, H, HD), axis=-1)).T[:, :, None]
        exact_probs = jnp.exp(scores - logsum)
        grad_scores = exact_probs * (grad_probs - row_delta)
        per_offset = jax.ops.segment_sum(grad_scores.transpose(1, 2, 0).reshape(LEN * LEN, H), jnp.clip(offsets, 0, LEN - 1).reshape(LEN * LEN), num_segments=LEN)
        grad_table = jnp.dot(bucket_hot.T, per_offset, precision=lax.Precision.HIGHEST)
        grad_scores_half = round_half(grad_scores)
        grad_queries_full = jnp.einsum('hij,jhd->ihd', grad_scores_half, as_float(key_rows).reshape(LEN, H, HD)).reshape(LEN, D) * SCALE
        grad_keys_full = jnp.einsum('hij,ihd->jhd', grad_scores_half, as_float(queries).reshape(LEN, H, HD)).reshape(LEN, D)
        grad_query_half = as_half(grad_queries_full)
        grad_key_half = as_half(grad_keys_full)
        grad_value_half = as_half(grad_values_full)
        grad_w_query = jnp.dot(hidden_one.T, grad_query_half, preferred_element_type=jnp.float32)
        grad_w_key = jnp.dot(hidden_one.T, grad_key_half, preferred_element_type=jnp.float32)
        grad_w_value = jnp.dot(hidden_one.T, grad_value_half, preferred_element_type=jnp.float32)
        grad_hidden_one = jnp.dot(grad_query_half, w_query.T, preferred_element_type=jnp.float32)
        grad_hidden_one = grad_hidden_one + jnp.dot(grad_key_half, w_key.T, preferred_element_type=jnp.float32)
        grad_hidden_one = grad_hidden_one + jnp.dot(grad_value_half, w_value.T, preferred_element_type=jnp.float32)
        moved_one, grad_gain_one = rms_back(grad_hidden_one, unit_one, inv_one, as_float(attn_gain))
        pieces = (grad_w_query, grad_w_key, grad_w_value, grad_w_output, grad_gain_one, grad_table)
        new_totals = tuple((total + piece for total, piece in zip(totals, pieces)))
        return (new_totals, grad_mix + moved_one)
    initial = (jnp.zeros((D, D), jnp.float32), jnp.zeros((D, D), jnp.float32), jnp.zeros((D, D), jnp.float32), jnp.zeros((D, D), jnp.float32), jnp.zeros((D,), jnp.float32), jnp.zeros((NB, H), jnp.float32))
    totals, input_grad = lax.scan(seq_back, initial, (block_input, grad_mixed))
    grad_query, grad_key, grad_value, grad_output, grad_attn_gain, grad_bias_table = totals
    return (block_output.reshape(SEQS, LEN, D), input_grad, grad_query, grad_key, grad_value, grad_output, grad_router, grad_attn_gain, grad_moe_gain, grad_bias_table, grad_expert_in, grad_expert_out)
```

```python
import functools
import math

import jax
import jax.numpy as jnp
import numpy as np
from jax import lax
from jax.experimental import pallas as pl
from jax.experimental.pallas import tpu as pltpu
from jax.sharding import PartitionSpec as P

HD = 64
CAP = 6
TILE = 128
EXTRA = 128
HALVES = 2

EPS = 1e-06
SCALE = 0.125
INV_ROOT_TWO = 1.0 / math.sqrt(2.0)
INV_ROOT_TAU = 1.0 / math.sqrt(2.0 * math.pi)
NEG = -1e30

NN = (((1,), (0,)), ((), ()))
NT = (((1,), (1,)), ((), ()))
TN = (((0,), (0,)), ((), ()))


VMEM = pl.BlockSpec(memory_space=pltpu.VMEM)
SMEM = pl.BlockSpec(memory_space=pltpu.SMEM)


def f32(x):
    return x.astype(jnp.float32)


def b16(x):
    return x.astype(jnp.bfloat16)


def dot(a, b, dims=NN, precision=None):
    return lax.dot_general(a, b, dims, precision=precision, preferred_element_type=jnp.float32)


def iota(shape, axis):
    return lax.broadcasted_iota(jnp.int32, shape, axis)


def call(kernel, args, outs, scratch=(), flops=1e8, n_smem=1, name=None):
    size = sum(int(np.prod(a.shape)) * a.dtype.itemsize for a in args)
    size += sum(int(np.prod(s)) * jnp.dtype(d).itemsize for s, d in outs)
    return pl.pallas_call(
        kernel,
        out_shape=[jax.ShapeDtypeStruct(s, d) for s, d in outs],
        in_specs=[SMEM] * n_smem + [VMEM] * (len(args) - n_smem),
        out_specs=[VMEM] * len(outs),
        scratch_shapes=list(scratch),
        cost_estimate=pl.CostEstimate(flops=int(flops), bytes_accessed=size, transcendentals=0),
        name=name,
    )(*args)


def assemble(idx_ref, pieces, target, rows):
    if len(pieces) == 1:
        target[0 : pieces[0].shape[0], :] = pieces[0][...]
        return
    own = idx_ref[1]
    for order, piece in pieces:
        for n, off in enumerate(order):
            start = pl.multiple_of((own ^ off) * rows, rows)
            target[pl.ds(start, rows), :] = piece[n * rows : (n + 1) * rows, :]


def rms(x):
    inverse = lax.rsqrt(jnp.mean(x * x, axis=-1, keepdims=True) + EPS)
    return x * inverse, inverse


def table_select(buckets, width, rows, shards):
    per = buckets // shards
    b = iota((buckets, width), 0)
    shard = sum(((b >= per * s).astype(jnp.int32) for s in range(1, shards)), jnp.zeros_like(b))
    return iota((buckets, width), 1) == shard * rows + (b - shard * per)


def attn_forward(cfg, idx_ref, x_ref, bucket_ref, *refs):
    n_in = len(cfg.orders)
    pieces = refs[:n_in]
    q_ref, k_ref, v_ref, hid_ref, att_ref, lse_ref, bias_ref, w_ref, gain_ref, ah_ref = refs[n_in:]
    assemble(idx_ref, cfg.pair(pieces), w_ref, cfg.rows)
    D, S, hl, CQ = cfg.D, cfg.S, cfg.hl, cfg.CQ
    extra = w_ref[:, 3 * CQ :]
    ew = extra.shape[1]
    pick = b16((iota((16, ew), 0) == iota((16, ew), 1)).astype(jnp.float32))
    gain_rows = dot(pick, extra, NT)
    gain_ref[...] = gain_rows[0:8]
    unit, _ = rms(f32(x_ref[...]))
    hidden = b16(unit * gain_rows[0:1])
    hid_ref[...] = hidden
    qkv = dot(hidden, w_ref[:, : 3 * CQ])
    for h in range(hl):
        q_ref[h] = b16(qkv[:, h * HD : (h + 1) * HD] * SCALE)
        k_ref[h] = b16(qkv[:, CQ + h * HD : CQ + (h + 1) * HD])
        v_ref[h] = b16(qkv[:, 2 * CQ + h * HD : 2 * CQ + (h + 1) * HD])
    table = dot(b16(table_select(cfg.NB, D, cfg.rows, cfg.NE).astype(jnp.float32)), extra)
    lane, col = iota((ew, 16), 0), iota((ew, 16), 1)
    head = idx_ref[0] * hl + col
    mine = (lane == 2 + head) & (col < hl) & (head < cfg.H)
    table = dot(b16(table), b16(mine.astype(jnp.float32)))
    hot = b16((iota((cfg.NB, S), 0) == bucket_ref[...]).astype(jnp.float32))
    offset_bias = dot(b16(table), hot, TN)
    nb = S // TILE
    keep = iota((TILE, TILE), 0) >= iota((TILE, TILE), 1)
    for h in range(hl):
        for k in range(nb):
            now = offset_bias[h : h + 1, k * TILE : (k + 1) * TILE]
            before = offset_bias[h : h + 1, (k - 1) * TILE : k * TILE] if k else now
            row = jnp.concatenate([now, before], axis=1)
            turned = pltpu.roll(
                jnp.broadcast_to(row, (TILE, 2 * TILE)), 0, 1, stride=1, stride_axis=0
            )
            tile = jnp.transpose(turned[:, :TILE])
            bias_ref[h, k] = jnp.where(keep, tile, NEG) if k == 0 else tile

    def one_head(h, carry):
        for ib in range(nb):
            n = (ib + 1) * TILE
            s = dot(q_ref[h, ib * TILE : n], k_ref[h, 0:n], NT)
            s = s + jnp.concatenate([bias_ref[h, ib - jb] for jb in range(ib + 1)], axis=1)
            peak = jnp.max(s, axis=1, keepdims=True)
            lse = peak + jnp.log(jnp.sum(jnp.exp(s - peak), axis=1, keepdims=True))
            lse_ref[h, ib * TILE : n] = lse
            ah_ref[h, ib * TILE : n] = dot(b16(jnp.exp(s - lse)), v_ref[h, 0:n])
        return carry

    lax.fori_loop(0, hl, one_head, 0)
    for h in range(hl):
        att_ref[:, h * HD : (h + 1) * HD] = b16(ah_ref[h])


def slots_of(ids, experts):
    n = ids.shape[0]
    first, second = ids[:, 0:1], ids[:, 1:2]
    e = iota((n, experts), 1)
    hot_a, hot_b = (e == first).astype(jnp.float32), (e == second).astype(jnp.float32)
    earlier = (iota((n, n), 0) > iota((n, n), 1)).astype(jnp.float32)
    count = dot(b16(earlier), b16(hot_a + hot_b))
    slot_a = first * CAP + jnp.sum(count * hot_a, axis=1, keepdims=True).astype(jnp.int32)
    slot_b = second * CAP + jnp.sum(count * hot_b, axis=1, keepdims=True).astype(jnp.int32)
    return slot_a, slot_b


def hot_slots(slot, start, width):
    return (slot == start + iota((slot.shape[0], width), 1)).astype(jnp.float32)


def send_upstream(cfg, idx_ref, ids_ref, up_ref, *outs):
    ids = ids_ref[...]
    slot_a, slot_b = slots_of(ids, cfg.E)
    n = cfg.XC
    other_a = b16(jnp.broadcast_to(f32(ids[:, 1:2]), (cfg.B, EXTRA)))
    other_b = b16(jnp.broadcast_to(f32(ids[:, 0:1]), (cfg.B, EXTRA)))
    for k in range(cfg.NE):
        start = (idx_ref[1] ^ k) * n
        hot_a, hot_b = hot_slots(slot_a, start, n), hot_slots(slot_b, start, n)
        outs[k][:, : cfg.D] = b16(dot(b16(hot_a + hot_b), up_ref[...], TN))
        outs[k][:, cfg.D :] = b16(dot(b16(hot_a), other_a, TN) + dot(b16(hot_b), other_b, TN))


def middle(cfg, idx_ref, att_ref, x_ref, ids_ref, gain_ref, *refs):
    n_in = len(cfg.orders)
    pieces = refs[:n_in]
    mixed_ref, wo_ref, router_ref = refs[n_in : n_in + 3]
    outs = refs[n_in + 3 : n_in + 3 + cfg.NE]
    w_ref = refs[-1]
    assemble(idx_ref, cfg.pair(pieces), w_ref, cfg.rows)
    D, CQ = cfg.D, cfg.CQ
    wo_ref[0:D, :] = w_ref[:, :D]
    if cfg.NC * CQ > D:
        wo_ref[D:, :] = jnp.zeros((cfg.NC * CQ - D, D), jnp.bfloat16)
    router_ref[...] = w_ref[:, D : D + cfg.E]
    mixed = f32(x_ref[...])
    for c in range(cfg.NC):
        start = pl.multiple_of(c * cfg.S + idx_ref[0] * cfg.B, cfg.B)
        mixed = mixed + dot(att_ref[pl.ds(start, cfg.B), :], wo_ref[c * CQ : (c + 1) * CQ, :])
    mixed_ref[...] = mixed
    unit, _ = rms(mixed)
    hidden = b16(unit * gain_ref[1:2, :])
    slot_a, slot_b = slots_of(ids_ref[...], cfg.E)
    n = cfg.XC
    for k in range(cfg.NE):
        start = (idx_ref[1] ^ k) * n
        hot = hot_slots(slot_a, start, n) + hot_slots(slot_b, start, n)
        outs[k][...] = b16(dot(b16(hot), hidden, TN))


def arrange(cfg, order_ref, *refs):
    pieces, outs = refs[: cfg.NE], refs[cfg.NE :]
    rows = jnp.concatenate([p[...] for p in pieces], axis=0)
    total = rows.shape[0]
    part = total // HALVES
    for n, out in enumerate(outs):
        hot = (iota((part, total), 0) + n * part == order_ref[...]).astype(jnp.float32)
        out[...] = b16(dot(b16(hot), rows))


def gather_sum(cfg, order_ref, *refs):
    ins, outs = refs[: HALVES * cfg.NC], refs[HALVES * cfg.NC :]
    halves = []
    for n in range(HALVES):
        group = ins[n * cfg.NC : (n + 1) * cfg.NC]
        total = f32(group[0][...])
        for piece in group[1:]:
            total = total + f32(piece[...])
        halves.append(b16(total))
    rows = jnp.concatenate(halves, axis=0)
    count = rows.shape[0]
    hot = (iota((count, count), 0) == order_ref[...]).astype(jnp.float32)
    back = b16(dot(b16(hot), rows, TN))
    for k, out in enumerate(outs):
        out[...] = back[k * cfg.XC : (k + 1) * cfg.XC]


def collect(cfg, idx_ref, ids, pieces):
    slot_a, slot_b = slots_of(ids, cfg.E)
    total = None
    for k, piece in enumerate(pieces):
        start = (idx_ref[1] ^ k) * cfg.XC
        hot = hot_slots(slot_a, start, cfg.XC) + hot_slots(slot_b, start, cfg.XC)
        term = dot(b16(hot), piece[...])
        total = term if total is None else total + term
    return total


def finish_forward(cfg, idx_ref, ids_ref, mixed_ref, *refs):
    refs[-1][...] = mixed_ref[...] + collect(cfg, idx_ref, ids_ref[...], refs[:-1])


def moe_back(cfg, idx_ref, ids_ref, mixed_ref, gain_ref, up_ref, *refs):
    pieces = refs[: cfg.NE]
    mix_ref, half_ref, gg_ref = refs[cfg.NE :]
    grad = collect(cfg, idx_ref, ids_ref[...], pieces)
    unit, inverse = rms(mixed_ref[...])
    gg_ref[...] = jnp.broadcast_to(jnp.sum(grad * unit, axis=0, keepdims=True), (8, cfg.D))
    scaled = grad * gain_ref[1:2, :]
    moved = inverse * (scaled - unit * jnp.mean(scaled * unit, axis=-1, keepdims=True))
    grad_mixed = f32(up_ref[...]) + moved
    mix_ref[...] = grad_mixed
    half_ref[...] = b16(grad_mixed)


def expert_kernel(cfg, first, n_alias, idx_ref, *refs):
    NC, D, E = cfg.NC, cfg.D, cfg.E
    rows_in, ups_in = refs[:NC], refs[NC : 2 * NC]
    win_ref, wout_ref, router_ref = refs[2 * NC : 2 * NC + 3]
    outs = refs[2 * NC + 3 + n_alias :]
    back, fwd = outs[:NC], outs[NC : 2 * NC]
    rows_out, up_out, act_out, pre_out, route_out = outs[2 * NC :]
    step = pl.program_id(0)
    own = idx_ref[1] * cfg.X + first + step
    rows = jnp.concatenate([r[...] for r in rows_in], axis=0)
    ups = jnp.concatenate([u[...] for u in ups_in], axis=0)
    count = rows.shape[0]
    win, wout = win_ref[0], wout_ref[0]
    other = ups[:, D : D + 1].astype(jnp.float32).astype(jnp.int32)
    up = f32(ups[:, :D])
    lane = iota((count, E), 1)
    is_own = (lane == own).astype(jnp.float32)
    is_other = (lane == other).astype(jnp.float32)
    sign = is_own - is_other
    gap = jnp.sum(dot(rows, router_ref[...]) * sign, axis=1, keepdims=True)
    gate = jax.nn.sigmoid(gap)
    against = jax.nn.sigmoid(-gap)
    up_rows = b16(gate * up)
    preact = dot(rows, win)
    cdf = 0.5 * (1.0 + lax.erf(preact * INV_ROOT_TWO))
    slope = cdf + preact * jnp.exp(-0.5 * preact * preact) * INV_ROOT_TAU
    active = b16(preact * cdf)
    part = dot(active, wout)
    grad_pre = b16(dot(up_rows, wout, NT) * slope)
    weight = gate * against * jnp.sum(up * part, axis=1, keepdims=True)
    coef = weight * sign
    high = b16(coef)
    low = b16(coef - f32(high))
    route_ref = router_ref[...]
    both = jnp.concatenate([f32(high), f32(low)], axis=1).astype(jnp.bfloat16)
    wide = jnp.concatenate([f32(route_ref), f32(route_ref)], axis=1).astype(jnp.bfloat16)
    back_rows = dot(grad_pre, win, NT) + dot(both, wide, NT)
    route = dot(rows, both, TN)

    @pl.when(step == 0)
    def _():
        route_out[...] = route

    @pl.when(step > 0)
    def _():
        route_out[...] += route

    fwd_rows = b16(gate * part)
    back_rows = b16(back_rows)
    each = count // NC
    for c in range(NC):
        back[c][...] = back_rows[c * each : (c + 1) * each]
        fwd[c][...] = fwd_rows[c * each : (c + 1) * each]
    rows_out[0] = rows
    up_out[0] = up_rows
    act_out[0] = active
    pre_out[0] = grad_pre


def experts(cfg, half, idx, rows, ups, w_in, w_out, router, earlier):
    NC, D, FL = cfg.NC, cfg.D, w_in.shape[2]
    steps = cfg.X // HALVES
    first = half * steps
    each = cfg.NE * CAP
    count = NC * each
    fixed = lambda shape: pl.BlockSpec(shape, lambda s: (0,) * len(shape))
    row = lambda w: pl.BlockSpec((each, w), lambda s: (s, 0))
    per = lambda a, b: pl.BlockSpec((1, a, b), lambda s: (first + s, 0, 0))
    saved = [((cfg.X, count, w), jnp.bfloat16) for w in (D, D, FL, FL)]
    outs = [((steps * each, D), jnp.bfloat16)] * (2 * NC) + saved + [((D, 2 * cfg.E), jnp.float32)]
    in_specs = [SMEM] + [row(D)] * NC + [row(D + EXTRA)] * NC
    in_specs += [per(D, FL), per(FL, D), fixed((D, cfg.E))]
    in_specs += [pl.BlockSpec(memory_space=pl.ANY)] * len(earlier)
    out_specs = [row(D)] * (2 * NC) + [per(count, w) for w in (D, D, FL, FL)]
    out_specs += [fixed((D, 2 * cfg.E))]
    base = 2 * NC + 4
    return pl.pallas_call(
        functools.partial(expert_kernel, cfg, first, len(earlier)),
        grid=(steps,),
        out_shape=[jax.ShapeDtypeStruct(s, d) for s, d in outs],
        in_specs=in_specs,
        out_specs=out_specs,
        input_output_aliases={base + n: 2 * NC + n for n in range(len(earlier))},
        cost_estimate=pl.CostEstimate(
            flops=steps * 4 * 2 * count * D * FL, bytes_accessed=steps * 4 * D * FL, transcendentals=0
        ),
        name=f"experts{half}",
    )(idx, *rows, *ups, w_in, w_out, router, *earlier)


def expert_weights_kernel(rows_ref, up_ref, act_ref, pre_ref, gin_ref, gout_ref):
    gin_ref[0] = dot(rows_ref[0], pre_ref[0], TN)
    gout_ref[0] = dot(act_ref[0], up_ref[0], TN)


def expert_weights(cfg, rows, up, act, pre):
    X, count, D = rows.shape
    FL = act.shape[2]
    per = lambda a, b: pl.BlockSpec((1, a, b), lambda s: (s, 0, 0))
    return pl.pallas_call(
        expert_weights_kernel,
        grid=(X,),
        out_shape=[
            jax.ShapeDtypeStruct((X, D, FL), jnp.float32),
            jax.ShapeDtypeStruct((X, FL, D), jnp.float32),
        ],
        in_specs=[per(count, D), per(count, D), per(count, FL), per(count, FL)],
        out_specs=[per(D, FL), per(FL, D)],
        cost_estimate=pl.CostEstimate(
            flops=X * 4 * count * D * FL, bytes_accessed=X * 8 * D * FL, transcendentals=0
        ),
        name="expert_weights",
    )(rows, up, act, pre)


def attn_backward(
    cfg, idx_ref, x_ref, bucket_ref, gm_ref, att_ref, wo_ref, q_ref, k_ref, v_ref, hid_ref, lse_ref,
    bias_ref, w_ref, gain_ref, gg_ref, *refs,
):
    routes = refs[:HALVES]
    mine_ref, part_ref, gh_ref, da_ref, dq_ref, dk_ref, dv_ref, p_ref, ds_ref, acc_ref, dw_ref = refs[HALVES:]
    D, S, hl, CQ, CO, B = cfg.D, cfg.S, cfg.hl, cfg.CQ, cfg.CO, cfg.B
    nb = S // TILE
    c = idx_ref[0]
    gm = gm_ref[...]
    own = pl.multiple_of(c * CQ, CQ)
    base = c * S
    grad_att = b16(dot(gm, wo_ref[pl.ds(own, CQ), :], NT))
    for h in range(hl):
        da_ref[h] = grad_att[:, h * HD : (h + 1) * HD]
    att_own = att_ref[pl.ds(pl.multiple_of(base, S), S), :]
    prod = f32(grad_att) * f32(att_own)
    deltas = [jnp.sum(prod[:, h * HD : (h + 1) * HD], axis=1, keepdims=True) for h in range(hl)]
    acc_ref[...] = jnp.zeros_like(acc_ref)
    for ib in range(nb):
        if ib + 1 < nb:
            zero = jnp.zeros((TILE, S - (ib + 1) * TILE), jnp.bfloat16)
            p_ref[ib * TILE : (ib + 1) * TILE, (ib + 1) * TILE :] = zero
            ds_ref[ib * TILE : (ib + 1) * TILE, (ib + 1) * TILE :] = zero
    for h in range(hl):
        for ib in range(nb):
            lo, n = ib * TILE, (ib + 1) * TILE
            s = dot(q_ref[h, lo:n], k_ref[h, 0:n], NT)
            s = s + jnp.concatenate([bias_ref[h, ib - jb] for jb in range(ib + 1)], axis=1)
            prob = jnp.exp(s - lse_ref[h, lo:n])
            grad_p = dot(da_ref[h, lo:n], v_ref[h, 0:n], NT)
            grad_s = prob * (grad_p - deltas[h][lo:n])
            p_ref[lo:n, 0:n] = b16(prob)
            half = b16(grad_s)
            ds_ref[lo:n, 0:n] = half
            dq_ref[h, lo:n] = dot(half, k_ref[h, 0:n]) * SCALE
            for jb in range(ib + 1):
                acc_ref[h, ib - jb] += grad_s[:, jb * TILE : (jb + 1) * TILE]
        dk_ref[h] = dot(ds_ref[...], q_ref[h], TN)
        dv_ref[h] = dot(p_ref[...], da_ref[h], TN)
    per_offset = []
    zero_tile = jnp.zeros((TILE, TILE), jnp.float32)
    sub = iota((8, 2 * TILE), 0)
    for h in range(hl):
        rows = []
        for k in range(nb):
            wide = jnp.concatenate([jnp.transpose(acc_ref[h, k]), zero_tile], axis=1)
            total = wide[0:8]
            for g in range(1, TILE // 8):
                total = total + pltpu.roll(wide[g * 8 : (g + 1) * 8], 2 * TILE - 8 * g, 1)
            for bit in (1, 2, 4):
                total = jnp.where((sub & bit) != 0, pltpu.roll(total, 2 * TILE - bit, 1), total)
            rows.append(jnp.sum(total, axis=0, keepdims=True))
        spans = []
        for k in range(nb):
            span = rows[k][:, :TILE]
            if k + 1 < nb:
                span = span + rows[k + 1][:, TILE:]
            spans.append(span)
        per_offset.append(jnp.concatenate(spans, axis=1))
    per_offset.append(jnp.zeros((8 - hl, S), jnp.float32))
    per_offset = jnp.concatenate(per_offset, axis=0)
    hot = (iota((cfg.NB, S), 0) == bucket_ref[...]).astype(jnp.float32)
    table = dot(per_offset, hot, NT, lax.Precision.HIGHEST)
    place = table_select(cfg.NB, D, cfg.rows, cfg.NE).astype(jnp.float32)
    table_rows = dot(table, place, NN, lax.Precision.HIGHEST)
    grads = jnp.concatenate(
        [dq_ref[h] for h in range(hl)] + [dk_ref[h] for h in range(hl)] + [dv_ref[h] for h in range(hl)],
        axis=1,
    )
    grads = b16(grads)
    dw_ref[:, : 3 * CQ] = dot(hid_ref[...], grads, TN)
    sel = b16((iota((D, CO), 0) == c * CO + iota((D, CO), 1)).astype(jnp.float32))
    gm_cols = b16(dot(gm, sel))
    for n in range(cfg.NC):
        lo, hi = n * CQ, min((n + 1) * CQ, D)
        if hi > lo:
            piece = dot(att_ref[n * S : (n + 1) * S, :], gm_cols, TN)
            dw_ref[lo:hi, 3 * CQ : 3 * CQ + CO] = piece[: hi - lo]
    gh = dot(grads, w_ref[:, : 3 * CQ], NT)
    gh_ref[...] = b16(gh)
    unit, _ = rms(f32(x_ref[...]))
    gain_one = jnp.sum(gh * unit, axis=0, keepdims=True)
    E = cfg.E
    stack = jnp.concatenate(
        [
            jnp.zeros((E, D), jnp.float32),
            gain_one,
            gg_ref[0:1, :],
            table_rows[0:hl],
            jnp.zeros((EXTRA - E - 2 - hl, D), jnp.float32),
        ],
        axis=0,
    )
    extra = jnp.transpose(stack)
    route = routes[0][...]
    for r in routes[1:]:
        route = route + r[...]
    route = route[:, :E] + route[:, E:]
    extra = extra + jnp.concatenate([route, jnp.zeros((D, EXTRA - E), jnp.float32)], axis=1)
    dw_ref[:, 3 * CQ + CO :] = extra
    me = idx_ref[1]
    R = cfg.rows
    for j in range(cfg.NE // 2):
        a = pl.multiple_of((me ^ (2 * j)) * R, R)
        b = pl.multiple_of((me ^ (2 * j + 1)) * R, R)
        mine_ref[j * R : (j + 1) * R, :] = b16(dw_ref[pl.ds(a, R), :])
        part_ref[j * R : (j + 1) * R, :] = b16(dw_ref[pl.ds(b, R), :])


def add_pairs(cfg, a_ref, b_ref, *outs):
    R = cfg.rows
    for j, out in enumerate(outs):
        out[...] = b16(f32(a_ref[j * R : (j + 1) * R]) + f32(b_ref[j * R : (j + 1) * R]))


def add_all(*refs):
    total = f32(refs[0][...])
    for r in refs[1:-1]:
        total = total + f32(r[...])
    refs[-1][...] = b16(total)


def last_input(cfg, gh_ref, x_ref, gain_ref, mix_ref, out_ref):
    B = cfg.B
    total = f32(gh_ref[0:B])
    for n in range(1, cfg.NC):
        total = total + f32(gh_ref[n * B : (n + 1) * B])
    unit, inverse = rms(f32(x_ref[...]))
    scaled = total * gain_ref[0:1, :]
    moved = inverse * (scaled - unit * jnp.mean(scaled * unit, axis=-1, keepdims=True))
    out_ref[...] = mix_ref[...] + moved


def last_weights(cfg, all_ref, q_ref, k_ref, v_ref, o_ref, router_ref, gains_ref, table_ref):
    R, CQ, CO, D, hl, E = cfg.rows, cfg.CQ, cfg.CO, cfg.D, cfg.hl, cfg.E
    pieces = [f32(all_ref[n * R : (n + 1) * R, :]) for n in range(cfg.NC)]
    for t, ref in enumerate((q_ref, k_ref, v_ref)):
        full = jnp.concatenate([p[:, t * CQ : (t + 1) * CQ] for p in pieces], axis=1)
        ref[...] = full[:, :D]
    o_ref[...] = jnp.concatenate([p[:, 3 * CQ : 3 * CQ + CO] for p in pieces], axis=1)
    base = 3 * CQ + CO
    extra = pieces[0][:, base:]
    for p in pieces[1:]:
        extra = extra + p[:, base:]
    router_ref[...] = extra[:, :E]
    gains_ref[...] = extra[:, E : E + 2]
    table = jnp.concatenate([p[:, base + E + 2 : base + E + 2 + hl] for p in pieces], axis=1)
    table_ref[...] = table[: cfg.NB // cfg.NE, : cfg.H]


class Config:
    def pair(self, pieces):
        if len(pieces) == 1:
            return list(pieces)
        return list(zip(self.orders, pieces, strict=True))


def permute(x, axis, k, n):
    return lax.ppermute(x, axis, [(i, i ^ k) for i in range(n)])


def gather_rows(cfg, x):
    if len(cfg.orders) == 1:
        return [lax.all_gather(x, "ep", axis=0, tiled=True)]
    got = [x] + [permute(x, "ep", 2 * j, cfg.NE) for j in range(1, cfg.NE // 2)]
    return got + [permute(g, "ep", 1, cfg.NE) for g in got]


def body(
    block_input, out_grad, w_query, w_key, w_value, w_output, w_router, attn_gain, moe_gain,
    bias_table, rel_bucket, expert_ids, expert_in, expert_out,
):
    cfg = Config()
    NC, NE = lax.axis_size("ctx"), lax.axis_size("ep")
    B, D = block_input.shape[1:]
    S = rel_bucket.shape[0]
    cfg.NC, cfg.NE, cfg.B, cfg.D, cfg.S = NC, NE, B, D, S
    cfg.H = D // HD
    cfg.hl = -(-cfg.H // NC)
    cfg.CQ = CQ = cfg.hl * HD
    cfg.CO = CO = D // NC
    cfg.rows = R = D // NE
    cfg.X = X = expert_in.shape[0]
    cfg.E = E = X * NE
    cfg.XC = X * CAP
    cfg.NB = bias_table.shape[0] * NE
    hl = cfg.hl
    if R % 16 == 0:
        cfg.orders = [(2 * j,) for j in range(NE // 2)] + [(2 * j + 1,) for j in range(NE // 2)]
    else:
        cfg.orders = [None]
    bf, fl = jnp.bfloat16, jnp.float32
    c, e = lax.axis_index("ctx"), lax.axis_index("ep")
    idx = jnp.stack([c, e]).astype(jnp.int32)
    x_own, up_own, ids = block_input[0], out_grad[0], expert_ids[0]
    bucket = rel_bucket.reshape(1, S)

    def columns(w):
        w = jnp.pad(w, ((0, 0), (0, NC * CQ - D)))
        return lax.dynamic_slice_in_dim(w, c * CQ, CQ, 1)

    table = jnp.pad(bias_table, ((0, R - bias_table.shape[0]), (0, HD - 2 - cfg.H)))
    pack = jnp.concatenate(
        [columns(w_query), columns(w_key), columns(w_value), attn_gain[:, None], moe_gain[:, None], table],
        axis=1,
    )
    W1 = 3 * CQ + HD
    first = gather_rows(cfg, pack)
    x_all = lax.all_gather(x_own, "ctx", axis=0, tiled=True)
    second = gather_rows(cfg, jnp.concatenate([w_output, w_router], axis=1))
    up_send = call(
        functools.partial(send_upstream, cfg), [idx, ids, up_own], [((cfg.XC, D + EXTRA), bf)] * NE,
        name="send_upstream",
    )
    ks = np.arange(E * CAP)
    to = (ks % cfg.XC) // CAP * (NE * CAP) + ks // cfg.XC * CAP + ks % CAP
    order = jnp.asarray(to.reshape(1, -1), jnp.int32)

    def to_experts(sent):
        got = [sent[0]] + [permute(sent[k], "ep", k, NE) for k in range(1, NE)]
        w = sent[0].shape[1]
        halves = call(
            functools.partial(arrange, cfg), [order, *got], [((E * CAP // HALVES, w), bf)] * HALVES,
            n_smem=0, name="arrange",
        )
        return [[h] + [permute(h, "ctx", k, NC) for k in range(1, NC)] for h in halves]

    def from_experts(parts):
        got = []
        for half in parts:
            got += [half[0]] + [permute(half[k], "ctx", k, NC) for k in range(1, NC)]
        sent = call(
            functools.partial(gather_sum, cfg), [order, *got], [((cfg.XC, D), bf)] * NE, n_smem=0,
            name="gather_sum",
        )
        return [sent[0]] + [permute(sent[k], "ep", k, NE) for k in range(1, NE)]

    ups = to_experts(up_send)
    nb = S // TILE
    q, k, v, hidden, att, lse, bias, w_all, gains = call(
        functools.partial(attn_forward, cfg), [idx, x_all, bucket, *first],
        [((hl, S, HD), bf)] * 3 + [((S, D), bf), ((S, CQ), bf), ((hl, S, 1), fl), ((hl, nb, TILE, TILE), fl),
         ((D, W1), bf), ((8, D), fl)],
        scratch=[pltpu.VMEM((hl, S, HD), fl)], flops=2e9, name="attn_forward",
    )
    att_all = lax.all_gather(att, "ctx", axis=0, tiled=True)
    mixed, wo, router, *sent = call(
        functools.partial(middle, cfg), [idx, att_all, x_own, ids, gains, *second],
        [((B, D), fl), ((NC * CQ, D), bf), ((D, E), bf)] + [((cfg.XC, D), bf)] * NE,
        scratch=[pltpu.VMEM((D, D + E), bf)], name="middle",
    )
    rows = to_experts(sent)
    saved, backs, fwds, routes = [], [], [], []
    for half in range(HALVES):
        got = experts(cfg, half, idx, rows[half], ups[half], expert_in, expert_out, router, saved)
        backs.append(got[:NC])
        fwds.append(got[NC : 2 * NC])
        saved = got[2 * NC : 2 * NC + 4]
        routes.append(got[-1])
    back = from_experts(backs)
    grad_expert_in, grad_expert_out = expert_weights(cfg, *saved)
    mix, mix_half, gg = call(
        functools.partial(moe_back, cfg), [idx, ids, mixed, gains, up_own, *back],
        [((B, D), fl), ((B, D), bf), ((8, D), fl)], name="moe_back",
    )
    fwd = from_experts(fwds)
    (block_output,) = call(
        functools.partial(finish_forward, cfg), [idx, ids, mixed, *fwd], [((B, D), fl)], name="finish_forward"
    )
    gm_all = lax.all_gather(mix_half, "ctx", axis=0, tiled=True)
    WC = 3 * CQ + CO + EXTRA
    mine, part, gh = call(
        functools.partial(attn_backward, cfg),
        [idx, x_all, bucket, gm_all, att_all, wo, q, k, v, hidden, lse, bias, w_all, gains, gg, *routes],
        [((D // 2, WC), bf)] * 2 + [((S, D), bf)],
        scratch=[
            pltpu.VMEM((hl, S, HD), bf),
            pltpu.VMEM((hl, S, HD), fl),
            pltpu.VMEM((hl, S, HD), fl),
            pltpu.VMEM((hl, S, HD), fl),
            pltpu.VMEM((S, S), bf),
            pltpu.VMEM((S, S), bf),
            pltpu.VMEM((hl, nb, TILE, TILE), fl),
            pltpu.VMEM((D, WC), fl),
        ],
        flops=4e9, name="attn_backward",
    )
    gh_all = lax.all_to_all(gh, "ctx", split_axis=0, concat_axis=0, tiled=True)
    theirs = permute(part, "ep", 1, NE)
    pairs = call(
        functools.partial(add_pairs, cfg), [mine, theirs], [((R, WC), bf)] * (NE // 2), n_smem=0, name="add_pairs"
    )
    pairs = [pairs[0]] + [permute(pairs[j], "ep", 2 * j, NE) for j in range(1, NE // 2)]
    (total,) = call(add_all, pairs, [((R, WC), bf)], n_smem=0, name="add_all")
    everyone = lax.all_gather(total, "ctx", axis=0, tiled=True)
    (input_grad,) = call(
        functools.partial(last_input, cfg), [gh_all, x_own, gains, mix], [((B, D), fl)], n_smem=0, name="last_input"
    )
    nbl = bias_table.shape[0]
    gq, gk, gv, go, grouter, ggains, gtable = call(
        functools.partial(last_weights, cfg), [everyone],
        [((R, D), fl)] * 4 + [((R, E), fl), ((R, 2), fl), ((nbl, cfg.H), fl)], n_smem=0, name="last_weights",
    )
    return (
        block_output[None], input_grad[None], gq, gk, gv, go, grouter, ggains[:, 0], ggains[:, 1], gtable,
        grad_expert_in, grad_expert_out,
    )


def solution(mesh):
    two, three = P("ep", None), P("ep", "ctx", None)
    in_specs = (three, three, two, two, two, two, two, P("ep"), P("ep"), two, P(), three, P("ep", None, "ctx"), three)
    out_specs = (three, three, two, two, two, two, two, P("ep"), P("ep"), two, P("ep", None, "ctx"), three)
    return jax.shard_map(body, mesh=mesh, in_specs=in_specs, out_specs=out_specs, check_vma=False)
```

```python
import functools
import math

import jax
import jax.numpy as jnp
import numpy as np
from jax import lax
from jax.experimental import pallas as pl
from jax.experimental.pallas import tpu as pltpu
from jax.sharding import PartitionSpec as P


HD = 64
CAP = 6
TILE = 128
EXTRA = 128
HALVES = 2

EPS = 1e-06
SCALE = 0.125
INV_ROOT_TWO = 1.0 / math.sqrt(2.0)
INV_ROOT_TAU = 1.0 / math.sqrt(2.0 * math.pi)
NEG = -1e30

NN = (((1,), (0,)), ((), ()))
NT = (((1,), (1,)), ((), ()))
TN = (((0,), (0,)), ((), ()))


VMEM = pl.BlockSpec(memory_space=pltpu.VMEM)
SMEM = pl.BlockSpec(memory_space=pltpu.SMEM)


def f32(x):
    return x.astype(jnp.float32)


def b16(x):
    return x.astype(jnp.bfloat16)


def dot(a, b, dims=NN, precision=None):
    return lax.dot_general(a, b, dims, precision=precision, preferred_element_type=jnp.float32)


def iota(shape, axis):
    return lax.broadcasted_iota(jnp.int32, shape, axis)


def call(kernel, args, outs, scratch=(), flops=1e8, n_smem=1):
    size = sum(int(np.prod(a.shape)) * a.dtype.itemsize for a in args)
    size += sum(int(np.prod(s)) * jnp.dtype(d).itemsize for s, d in outs)
    return pl.pallas_call(
        kernel,
        out_shape=[jax.ShapeDtypeStruct(s, d) for s, d in outs],
        in_specs=[SMEM] * n_smem + [VMEM] * (len(args) - n_smem),
        out_specs=[VMEM] * len(outs),
        scratch_shapes=list(scratch),
        cost_estimate=pl.CostEstimate(flops=int(flops), bytes_accessed=size, transcendentals=0),
    )(*args)


def assemble(idx_ref, pieces, target, rows):
    if len(pieces) == 1:
        target[0 : pieces[0].shape[0], :] = pieces[0][...]
        return
    own = idx_ref[1]
    for order, piece in pieces:
        for n, off in enumerate(order):
            start = pl.multiple_of((own ^ off) * rows, rows)
            target[pl.ds(start, rows), :] = piece[n * rows : (n + 1) * rows, :]


def rms(x):
    inverse = lax.rsqrt(jnp.mean(x * x, axis=-1, keepdims=True) + EPS)
    return x * inverse, inverse


def table_select(buckets, width, rows, shards):
    per = buckets // shards
    b = iota((buckets, width), 0)
    shard = sum(((b >= per * s).astype(jnp.int32) for s in range(1, shards)), jnp.zeros_like(b))
    return iota((buckets, width), 1) == shard * rows + (b - shard * per)


def pack_weights(
    cfg, idx_ref, q_ref, k_ref, v_ref, o_ref, router_ref, one_ref, two_ref, table_ref, a_ref, b_ref, ext_ref
):
    R, CQ, D = cfg.rows, cfg.CQ, cfg.D
    width = cfg.NC * CQ
    shift = (cfg.NC - idx_ref[0]) * CQ
    for n, ref in enumerate((q_ref, k_ref, v_ref)):
        w = f32(ref[...])
        if width > D:
            w = jnp.concatenate([w, jnp.zeros((R, width - D), jnp.float32)], axis=1)
        a_ref[:, n * CQ : (n + 1) * CQ] = b16(pltpu.roll(w, shift, 1)[:, :CQ])
    ext_ref[...] = jnp.zeros_like(ext_ref)
    ext_ref[0 : table_ref.shape[0], 2 : 2 + cfg.H] = f32(table_ref[...])
    eye = (iota((R, R), 0) == iota((R, R), 1)).astype(jnp.float32)
    col_one = jnp.sum(eye * f32(one_ref[...]), axis=1, keepdims=True)
    col_two = jnp.sum(eye * f32(two_ref[...]), axis=1, keepdims=True)
    lane = iota((R, HD), 1)
    ext = ext_ref[:, :HD]
    ext = jnp.where(lane == 0, col_one, jnp.where(lane == 1, col_two, ext))
    a_ref[:, 3 * CQ :] = b16(ext)
    b_ref[:, :D] = o_ref[...]
    b_ref[:, D:] = b16(dot(b16(eye), router_ref[...], NT))


def place_blocks(cfg, idx_ref, pieces, target):
    for k, piece in enumerate(pieces):
        start = pl.multiple_of((idx_ref[0] ^ k) * cfg.B, cfg.B)
        target[pl.ds(start, cfg.B), :] = piece[...]


def attn_forward(cfg, idx_ref, bucket_ref, *refs):
    n_in = len(cfg.orders)
    pieces, refs = refs[:n_in], refs[n_in:]
    x_pieces, (x_ref, *refs) = refs[: cfg.NC], refs[cfg.NC :]
    place_blocks(cfg, idx_ref, x_pieces, x_ref)
    q_ref, k_ref, v_ref, hid_ref, att_ref, lse_ref, bias_ref, w_ref, gain_ref, ah_ref = refs
    assemble(idx_ref, cfg.pair(pieces), w_ref, cfg.rows)
    D, S, hl, CQ = cfg.D, cfg.S, cfg.hl, cfg.CQ
    extra = w_ref[:, 3 * CQ :]
    ew = extra.shape[1]
    pick = b16((iota((16, ew), 0) == iota((16, ew), 1)).astype(jnp.float32))
    gain_rows = dot(pick, extra, NT)
    gain_ref[...] = gain_rows[0:8]
    unit, _ = rms(f32(x_ref[...]))
    hidden = b16(unit * gain_rows[0:1])
    hid_ref[...] = hidden
    qkv = dot(hidden, w_ref[:, : 3 * CQ])
    for h in range(hl):
        q_ref[h] = b16(qkv[:, h * HD : (h + 1) * HD] * SCALE)
        k_ref[h] = b16(qkv[:, CQ + h * HD : CQ + (h + 1) * HD])
        v_ref[h] = b16(qkv[:, 2 * CQ + h * HD : 2 * CQ + (h + 1) * HD])
    table = dot(b16(table_select(cfg.NB, D, cfg.rows, cfg.NE).astype(jnp.float32)), extra)
    lane, col = iota((ew, 16), 0), iota((ew, 16), 1)
    head = idx_ref[0] * hl + col
    mine = (lane == 2 + head) & (col < hl) & (head < cfg.H)
    table = dot(b16(table), b16(mine.astype(jnp.float32)))
    hot = b16((iota((cfg.NB, S), 0) == bucket_ref[...]).astype(jnp.float32))
    offset_bias = dot(b16(table), hot, TN)
    nb = S // TILE
    keep = iota((TILE, TILE), 0) >= iota((TILE, TILE), 1)
    for h in range(hl):
        for k in range(nb):
            now = offset_bias[h : h + 1, k * TILE : (k + 1) * TILE]
            before = offset_bias[h : h + 1, (k - 1) * TILE : k * TILE] if k else now
            row = jnp.concatenate([now, before], axis=1)
            turned = pltpu.roll(
                jnp.broadcast_to(row, (TILE, 2 * TILE)), 0, 1, stride=1, stride_axis=0
            )
            tile = jnp.transpose(turned[:, :TILE])
            bias_ref[h, k] = jnp.where(keep, tile, NEG) if k == 0 else tile

    def one_head(h, carry):
        for ib in range(nb):
            n = (ib + 1) * TILE
            s = dot(q_ref[h, ib * TILE : n], k_ref[h, 0:n], NT)
            s = s + jnp.concatenate([bias_ref[h, ib - jb] for jb in range(ib + 1)], axis=1)
            peak = jnp.max(s, axis=1, keepdims=True)
            lse = peak + jnp.log(jnp.sum(jnp.exp(s - peak), axis=1, keepdims=True))
            lse_ref[h, ib * TILE : n] = lse
            ah_ref[h, ib * TILE : n] = dot(b16(jnp.exp(s - lse)), v_ref[h, 0:n])
        return carry

    lax.fori_loop(0, hl, one_head, 0)
    for h in range(hl):
        att_ref[:, h * HD : (h + 1) * HD] = b16(ah_ref[h])


def slots_of(ids, experts):
    n = ids.shape[0]
    first, second = ids[:, 0:1], ids[:, 1:2]
    e = iota((n, experts), 1)
    hot_a, hot_b = (e == first).astype(jnp.float32), (e == second).astype(jnp.float32)
    earlier = (iota((n, n), 0) > iota((n, n), 1)).astype(jnp.float32)
    count = dot(b16(earlier), b16(hot_a + hot_b))
    slot_a = first * CAP + jnp.sum(count * hot_a, axis=1, keepdims=True).astype(jnp.int32)
    slot_b = second * CAP + jnp.sum(count * hot_b, axis=1, keepdims=True).astype(jnp.int32)
    return slot_a, slot_b


def hot_slots(slot, start, width):
    return (slot == start + iota((slot.shape[0], width), 1)).astype(jnp.float32)


def send_upstream(cfg, idx_ref, ids_ref, up_ref, *outs):
    ids = ids_ref[...]
    slot_a, slot_b = slots_of(ids, cfg.E)
    n = cfg.XC
    other_a = b16(jnp.broadcast_to(f32(ids[:, 1:2]), (cfg.B, EXTRA)))
    other_b = b16(jnp.broadcast_to(f32(ids[:, 0:1]), (cfg.B, EXTRA)))
    for k in range(cfg.NE):
        start = (idx_ref[1] ^ k) * n
        hot_a, hot_b = hot_slots(slot_a, start, n), hot_slots(slot_b, start, n)
        outs[k][:, : cfg.D] = b16(dot(b16(hot_a + hot_b), up_ref[...], TN))
        outs[k][:, cfg.D :] = b16(dot(b16(hot_a), other_a, TN) + dot(b16(hot_b), other_b, TN))


def middle(cfg, idx_ref, x_ref, ids_ref, gain_ref, *refs):
    n_in = len(cfg.orders)
    atts, refs = refs[: cfg.NC], refs[cfg.NC :]
    pieces = refs[:n_in]
    mixed_ref, wo_ref, router_ref = refs[n_in : n_in + 3]
    outs = refs[n_in + 3 : n_in + 3 + cfg.NE]
    w_ref = refs[-1]
    assemble(idx_ref, cfg.pair(pieces), w_ref, cfg.rows)
    D, CQ = cfg.D, cfg.CQ
    wo_ref[0:D, :] = w_ref[:, :D]
    if cfg.NC * CQ > D:
        wo_ref[D:, :] = jnp.zeros((cfg.NC * CQ - D, D), jnp.bfloat16)
    router_ref[...] = w_ref[:, D : D + cfg.E]
    mixed = f32(x_ref[...])
    start = pl.multiple_of(idx_ref[0] * cfg.B, cfg.B)
    for k in range(cfg.NC):
        heads = pl.multiple_of((idx_ref[0] ^ k) * CQ, CQ)
        mixed = mixed + dot(atts[k][pl.ds(start, cfg.B), :], wo_ref[pl.ds(heads, CQ), :])
    mixed_ref[...] = mixed
    unit, _ = rms(mixed)
    hidden = b16(unit * gain_ref[1:2, :])
    slot_a, slot_b = slots_of(ids_ref[...], cfg.E)
    n = cfg.XC
    for k in range(cfg.NE):
        start = (idx_ref[1] ^ k) * n
        hot = hot_slots(slot_a, start, n) + hot_slots(slot_b, start, n)
        outs[k][...] = b16(dot(b16(hot), hidden, TN))


def arrange(cfg, order_ref, *refs):
    pieces, outs = refs[: cfg.NE], refs[cfg.NE :]
    rows = jnp.concatenate([p[...] for p in pieces], axis=0)
    total = rows.shape[0]
    part = total // HALVES
    for n, out in enumerate(outs):
        hot = (iota((part, total), 0) + n * part == order_ref[...]).astype(jnp.float32)
        out[...] = b16(dot(b16(hot), rows))


def gather_sum(cfg, order_ref, *refs):
    ins, outs = refs[: HALVES * cfg.NC], refs[HALVES * cfg.NC :]
    halves = []
    for n in range(HALVES):
        group = ins[n * cfg.NC : (n + 1) * cfg.NC]
        total = f32(group[0][...])
        for piece in group[1:]:
            total = total + f32(piece[...])
        halves.append(b16(total))
    rows = jnp.concatenate(halves, axis=0)
    count = rows.shape[0]
    hot = (iota((count, count), 0) == order_ref[...]).astype(jnp.float32)
    back = b16(dot(b16(hot), rows, TN))
    for k, out in enumerate(outs):
        out[...] = back[k * cfg.XC : (k + 1) * cfg.XC]


def collect(cfg, idx_ref, ids, pieces):
    slot_a, slot_b = slots_of(ids, cfg.E)
    total = None
    for k, piece in enumerate(pieces):
        start = (idx_ref[1] ^ k) * cfg.XC
        hot = hot_slots(slot_a, start, cfg.XC) + hot_slots(slot_b, start, cfg.XC)
        term = dot(b16(hot), piece[...])
        total = term if total is None else total + term
    return total


def finish_forward(cfg, idx_ref, ids_ref, mixed_ref, *refs):
    refs[-1][...] = mixed_ref[...] + collect(cfg, idx_ref, ids_ref[...], refs[:-1])


def moe_back(cfg, idx_ref, ids_ref, mixed_ref, gain_ref, up_ref, *refs):
    pieces = refs[: cfg.NE]
    mix_ref, half_ref, gg_ref = refs[cfg.NE :]
    grad = collect(cfg, idx_ref, ids_ref[...], pieces)
    unit, inverse = rms(mixed_ref[...])
    gg_ref[...] = jnp.broadcast_to(jnp.sum(grad * unit, axis=0, keepdims=True), (8, cfg.D))
    scaled = grad * gain_ref[1:2, :]
    moved = inverse * (scaled - unit * jnp.mean(scaled * unit, axis=-1, keepdims=True))
    grad_mixed = f32(up_ref[...]) + moved
    mix_ref[...] = grad_mixed
    half_ref[...] = b16(grad_mixed)


def expert_kernel(cfg, first, idx_ref, *refs):
    NC, D, E = cfg.NC, cfg.D, cfg.E
    rows_in, ups_in = refs[:NC], refs[NC : 2 * NC]
    win_ref, wout_ref, router_ref = refs[2 * NC : 2 * NC + 3]
    outs = refs[2 * NC + 3 :]
    back, fwd = outs[:NC], outs[NC : 2 * NC]
    rows_out, up_out, act_out, pre_out, route_out = outs[2 * NC :]
    step = pl.program_id(0)
    own = idx_ref[1] * cfg.X + first + step
    rows = jnp.concatenate([r[...] for r in rows_in], axis=0)
    ups = jnp.concatenate([u[...] for u in ups_in], axis=0)
    count = rows.shape[0]
    win, wout = win_ref[0], wout_ref[0]
    other = ups[:, D : D + 1].astype(jnp.float32).astype(jnp.int32)
    up = f32(ups[:, :D])
    lane = iota((count, E), 1)
    is_own = (lane == own).astype(jnp.float32)
    is_other = (lane == other).astype(jnp.float32)
    sign = is_own - is_other
    gap = jnp.sum(dot(rows, router_ref[...]) * sign, axis=1, keepdims=True)
    gate = jax.nn.sigmoid(gap)
    against = jax.nn.sigmoid(-gap)
    up_rows = b16(gate * up)
    preact = dot(rows, win)
    cdf = 0.5 * (1.0 + lax.erf(preact * INV_ROOT_TWO))
    slope = cdf + preact * jnp.exp(-0.5 * preact * preact) * INV_ROOT_TAU
    active = b16(preact * cdf)
    part = dot(active, wout)
    grad_pre = b16(dot(up_rows, wout, NT) * slope)
    weight = gate * against * jnp.sum(up * part, axis=1, keepdims=True)
    coef = weight * sign
    high = b16(coef)
    low = b16(coef - f32(high))
    route_ref = router_ref[...]
    both = jnp.concatenate([f32(high), f32(low)], axis=1).astype(jnp.bfloat16)
    wide = jnp.concatenate([f32(route_ref), f32(route_ref)], axis=1).astype(jnp.bfloat16)
    back_rows = dot(grad_pre, win, NT) + dot(both, wide, NT)
    route = dot(rows, both, TN)

    @pl.when(step == 0)
    def _():
        route_out[...] = route

    @pl.when(step > 0)
    def _():
        route_out[...] += route

    fwd_rows = b16(gate * part)
    back_rows = b16(back_rows)
    each = count // NC
    for c in range(NC):
        back[c][...] = back_rows[c * each : (c + 1) * each]
        fwd[c][...] = fwd_rows[c * each : (c + 1) * each]
    rows_out[0] = rows
    up_out[0] = up_rows
    act_out[0] = active
    pre_out[0] = grad_pre


def experts(cfg, half, idx, rows, ups, w_in, w_out, router):
    NC, D, FL = cfg.NC, cfg.D, w_in.shape[2]
    steps = cfg.X // HALVES
    first = half * steps
    each = cfg.NE * CAP
    count = NC * each
    fixed = lambda shape: pl.BlockSpec(shape, lambda s: (0,) * len(shape))
    row = lambda w: pl.BlockSpec((each, w), lambda s: (s, 0))
    per = lambda a, b: pl.BlockSpec((1, a, b), lambda s: (first + s, 0, 0))
    here = lambda a, b: pl.BlockSpec((1, a, b), lambda s: (s, 0, 0))
    saved = [((steps, count, w), jnp.bfloat16) for w in (D, D, FL, FL)]
    outs = [((steps * each, D), jnp.bfloat16)] * (2 * NC) + saved + [((D, 2 * cfg.E), jnp.float32)]
    in_specs = [SMEM] + [row(D)] * NC + [row(D + EXTRA)] * NC
    in_specs += [per(D, FL), per(FL, D), fixed((D, cfg.E))]
    out_specs = [row(D)] * (2 * NC) + [here(count, w) for w in (D, D, FL, FL)]
    out_specs += [fixed((D, 2 * cfg.E))]
    return pl.pallas_call(
        functools.partial(expert_kernel, cfg, first),
        grid=(steps,),
        out_shape=[jax.ShapeDtypeStruct(s, d) for s, d in outs],
        in_specs=in_specs,
        out_specs=out_specs,
        cost_estimate=pl.CostEstimate(
            flops=steps * 4 * 2 * count * D * FL, bytes_accessed=steps * 4 * D * FL, transcendentals=0
        ),
    )(idx, *rows, *ups, w_in, w_out, router)


def expert_weights_kernel(rows_ref, up_ref, act_ref, pre_ref, *refs):
    gin_ref, gout_ref = refs[-2:]
    gin_ref[0] = dot(rows_ref[0], pre_ref[0], TN)
    gout_ref[0] = dot(act_ref[0], up_ref[0], TN)


def expert_weights(cfg, half, rows, up, act, pre, earlier):
    steps, count, D = rows.shape
    FL = act.shape[2]
    here = lambda a, b: pl.BlockSpec((1, a, b), lambda s: (s, 0, 0))
    per = lambda a, b: pl.BlockSpec((1, a, b), lambda s: (half * steps + s, 0, 0))
    return pl.pallas_call(
        expert_weights_kernel,
        grid=(steps,),
        out_shape=[
            jax.ShapeDtypeStruct((cfg.X, D, FL), jnp.float32),
            jax.ShapeDtypeStruct((cfg.X, FL, D), jnp.float32),
        ],
        in_specs=[here(count, D), here(count, D), here(count, FL), here(count, FL)]
        + [pl.BlockSpec(memory_space=pl.ANY)] * len(earlier),
        out_specs=[per(D, FL), per(FL, D)],
        input_output_aliases={4 + n: n for n in range(len(earlier))},
        cost_estimate=pl.CostEstimate(
            flops=steps * 4 * count * D * FL, bytes_accessed=steps * 8 * D * FL, transcendentals=0
        ),
    )(rows, up, act, pre, *earlier)


def attn_backward(
    cfg, idx_ref, x_ref, bucket_ref, wo_ref, q_ref, k_ref, v_ref, hid_ref, lse_ref,
    bias_ref, w_ref, gain_ref, gg_ref, *refs,
):
    NC = cfg.NC
    routes, refs = refs[:HALVES], refs[HALVES:]
    gm_in, atts, refs = refs[:NC], refs[NC : 2 * NC], refs[2 * NC :]
    mine_ref, part_ref, *gh_out = refs[: 2 + NC]
    da_ref, dq_ref, dk_ref, dv_ref, p_ref, ds_ref, acc_ref, dw_ref, gm_ref, gh_ref = refs[2 + NC :]
    D, S, hl, CQ, CO, B = cfg.D, cfg.S, cfg.hl, cfg.CQ, cfg.CO, cfg.B
    nb = S // TILE
    c = idx_ref[0]
    place_blocks(cfg, idx_ref, gm_in, gm_ref)
    gm = gm_ref[...]
    own = pl.multiple_of(c * CQ, CQ)
    grad_att = b16(dot(gm, wo_ref[pl.ds(own, CQ), :], NT))
    for h in range(hl):
        da_ref[h] = grad_att[:, h * HD : (h + 1) * HD]
    prod = f32(grad_att) * f32(atts[0][...])
    deltas = [jnp.sum(prod[:, h * HD : (h + 1) * HD], axis=1, keepdims=True) for h in range(hl)]
    acc_ref[...] = jnp.zeros_like(acc_ref)
    for ib in range(nb):
        if ib + 1 < nb:
            zero = jnp.zeros((TILE, S - (ib + 1) * TILE), jnp.bfloat16)
            p_ref[ib * TILE : (ib + 1) * TILE, (ib + 1) * TILE :] = zero
            ds_ref[ib * TILE : (ib + 1) * TILE, (ib + 1) * TILE :] = zero
    for h in range(hl):
        for ib in range(nb):
            lo, n = ib * TILE, (ib + 1) * TILE
            s = dot(q_ref[h, lo:n], k_ref[h, 0:n], NT)
            s = s + jnp.concatenate([bias_ref[h, ib - jb] for jb in range(ib + 1)], axis=1)
            prob = jnp.exp(s - lse_ref[h, lo:n])
            grad_p = dot(da_ref[h, lo:n], v_ref[h, 0:n], NT)
            grad_s = prob * (grad_p - deltas[h][lo:n])
            p_ref[lo:n, 0:n] = b16(prob)
            half = b16(grad_s)
            ds_ref[lo:n, 0:n] = half
            dq_ref[h, lo:n] = dot(half, k_ref[h, 0:n]) * SCALE
            for jb in range(ib + 1):
                acc_ref[h, ib - jb] += grad_s[:, jb * TILE : (jb + 1) * TILE]
        dk_ref[h] = dot(ds_ref[...], q_ref[h], TN)
        dv_ref[h] = dot(p_ref[...], da_ref[h], TN)
    per_offset = []
    zero_tile = jnp.zeros((TILE, TILE), jnp.float32)
    sub = iota((8, 2 * TILE), 0)
    for h in range(hl):
        rows = []
        for k in range(nb):
            wide = jnp.concatenate([jnp.transpose(acc_ref[h, k]), zero_tile], axis=1)
            total = wide[0:8]
            for g in range(1, TILE // 8):
                total = total + pltpu.roll(wide[g * 8 : (g + 1) * 8], 2 * TILE - 8 * g, 1)
            for bit in (1, 2, 4):
                total = jnp.where((sub & bit) != 0, pltpu.roll(total, 2 * TILE - bit, 1), total)
            rows.append(jnp.sum(total, axis=0, keepdims=True))
        spans = []
        for k in range(nb):
            span = rows[k][:, :TILE]
            if k + 1 < nb:
                span = span + rows[k + 1][:, TILE:]
            spans.append(span)
        per_offset.append(jnp.concatenate(spans, axis=1))
    per_offset.append(jnp.zeros((8 - hl, S), jnp.float32))
    per_offset = jnp.concatenate(per_offset, axis=0)
    hot = (iota((cfg.NB, S), 0) == bucket_ref[...]).astype(jnp.float32)
    table = dot(per_offset, hot, NT, lax.Precision.HIGHEST)
    place = table_select(cfg.NB, D, cfg.rows, cfg.NE).astype(jnp.float32)
    table_rows = dot(table, place, NN, lax.Precision.HIGHEST)
    grads = jnp.concatenate(
        [dq_ref[h] for h in range(hl)] + [dk_ref[h] for h in range(hl)] + [dv_ref[h] for h in range(hl)],
        axis=1,
    )
    grads = b16(grads)
    dw_ref[0:D, : 3 * CQ] = dot(hid_ref[...], grads, TN)
    sel = b16((iota((D, CO), 0) == c * CO + iota((D, CO), 1)).astype(jnp.float32))
    gm_cols = b16(dot(gm, sel))
    for k in range(NC):
        heads = pl.multiple_of((c ^ k) * CQ, CQ)
        dw_ref[pl.ds(heads, CQ), 3 * CQ : 3 * CQ + CO] = dot(atts[k][...], gm_cols, TN)
    gh = dot(grads, w_ref[:, : 3 * CQ], NT)
    gh_ref[...] = b16(gh)
    for k, out in enumerate(gh_out):
        out[...] = gh_ref[pl.ds(pl.multiple_of((c ^ k) * B, B), B), :]
    unit, _ = rms(f32(x_ref[...]))
    gain_one = jnp.sum(gh * unit, axis=0, keepdims=True)
    E = cfg.E
    stack = jnp.concatenate(
        [
            jnp.zeros((E, D), jnp.float32),
            gain_one,
            gg_ref[0:1, :],
            table_rows[0:hl],
            jnp.zeros((EXTRA - E - 2 - hl, D), jnp.float32),
        ],
        axis=0,
    )
    extra = jnp.transpose(stack)
    route = routes[0][...]
    for r in routes[1:]:
        route = route + r[...]
    route = route[:, :E] + route[:, E:]
    extra = extra + jnp.concatenate([route, jnp.zeros((D, EXTRA - E), jnp.float32)], axis=1)
    dw_ref[0:D, 3 * CQ + CO :] = extra
    me = idx_ref[1]
    R = cfg.rows
    for j in range(cfg.NE // 2):
        a = pl.multiple_of((me ^ (2 * j)) * R, R)
        b = pl.multiple_of((me ^ (2 * j + 1)) * R, R)
        mine_ref[j * R : (j + 1) * R, :] = b16(dw_ref[pl.ds(a, R), :])
        part_ref[j * R : (j + 1) * R, :] = b16(dw_ref[pl.ds(b, R), :])


def add_pairs(cfg, a_ref, b_ref, *outs):
    R = cfg.rows
    for j, out in enumerate(outs):
        out[...] = b16(f32(a_ref[j * R : (j + 1) * R]) + f32(b_ref[j * R : (j + 1) * R]))


def add_all(*refs):
    total = f32(refs[0][...])
    for r in refs[1:-1]:
        total = total + f32(r[...])
    refs[-1][...] = b16(total)


def last_input(x_ref, gain_ref, mix_ref, *refs):
    out_ref = refs[-1]
    total = f32(refs[0][...])
    for ref in refs[1:-1]:
        total = total + f32(ref[...])
    unit, inverse = rms(f32(x_ref[...]))
    scaled = total * gain_ref[0:1, :]
    moved = inverse * (scaled - unit * jnp.mean(scaled * unit, axis=-1, keepdims=True))
    out_ref[...] = mix_ref[...] + moved


def last_weights(cfg, all_ref, q_ref, k_ref, v_ref, o_ref, router_ref, one_ref, two_ref, table_ref):
    R, CQ, CO, D, hl, E = cfg.rows, cfg.CQ, cfg.CO, cfg.D, cfg.hl, cfg.E
    pieces = [f32(all_ref[n * R : (n + 1) * R, :]) for n in range(cfg.NC)]
    for t, ref in enumerate((q_ref, k_ref, v_ref)):
        full = jnp.concatenate([p[:, t * CQ : (t + 1) * CQ] for p in pieces], axis=1)
        ref[...] = full[:, :D]
    o_ref[...] = jnp.concatenate([p[:, 3 * CQ : 3 * CQ + CO] for p in pieces], axis=1)
    base = 3 * CQ + CO
    extra = pieces[0][:, base:]
    for p in pieces[1:]:
        extra = extra + p[:, base:]
    router_ref[...] = jnp.transpose(extra)[:E]
    eye = (iota((R, R), 0) == iota((R, R), 1)).astype(jnp.float32)
    one_ref[...] = jnp.sum(eye * extra[:, E : E + 1], axis=0, keepdims=True)
    two_ref[...] = jnp.sum(eye * extra[:, E + 1 : E + 2], axis=0, keepdims=True)
    table = jnp.concatenate([p[:, base + E + 2 : base + E + 2 + hl] for p in pieces], axis=1)
    table_ref[...] = table[: cfg.NB // cfg.NE, : cfg.H]


class Config:
    def pair(self, pieces):
        if len(pieces) == 1:
            return list(pieces)
        return list(zip(self.orders, pieces, strict=True))


def permute(x, axis, k, n):
    return lax.ppermute(x, axis, [(i, i ^ k) for i in range(n)])


def spread(first, rest, axis, n):
    return [first] + [permute(x, axis, k, n) for k, x in zip(range(1, n), rest, strict=True)]


def gather_rows(cfg, x):
    if len(cfg.orders) == 1:
        return [lax.all_gather(x, "ep", axis=0, tiled=True)]
    got = [x] + [permute(x, "ep", 2 * j, cfg.NE) for j in range(1, cfg.NE // 2)]
    return got + [permute(g, "ep", 1, cfg.NE) for g in got]


def body(
    block_input, out_grad, w_query, w_key, w_value, w_output, w_router, attn_gain, moe_gain,
    bias_table, rel_bucket, expert_ids, expert_in, expert_out,
):
    cfg = Config()
    NC, NE = lax.axis_size("ctx"), lax.axis_size("ep")
    B, D = block_input.shape[1:]
    S = rel_bucket.shape[0]
    cfg.NC, cfg.NE, cfg.B, cfg.D, cfg.S = NC, NE, B, D, S
    cfg.H = D // HD
    cfg.hl = -(-cfg.H // NC)
    cfg.CQ = CQ = cfg.hl * HD
    cfg.CO = CO = D // NC
    cfg.rows = R = D // NE
    cfg.X = X = expert_in.shape[0]
    cfg.E = E = X * NE
    cfg.XC = X * CAP
    cfg.NB = bias_table.shape[0] * NE
    hl = cfg.hl
    if R % 16 == 0:
        cfg.orders = [(2 * j,) for j in range(NE // 2)] + [(2 * j + 1,) for j in range(NE // 2)]
    else:
        cfg.orders = [None]
    bf, fl = jnp.bfloat16, jnp.float32
    c, e = lax.axis_index("ctx"), lax.axis_index("ep")
    idx = jnp.stack([c, e]).astype(jnp.int32)
    x_own, up_own, ids = block_input[0], out_grad[0], expert_ids[0]
    bucket = rel_bucket.reshape(1, S)

    W1 = 3 * CQ + HD
    pack_a, pack_b = call(
        functools.partial(pack_weights, cfg),
        [idx, w_query, w_key, w_value, w_output, w_router.T, attn_gain[None], moe_gain[None], bias_table],
        [((R, W1), bf), ((R, D + E), bf)], scratch=[pltpu.VMEM((R, TILE), fl)],
    )
    first = gather_rows(cfg, pack_a)
    x_pieces = spread(x_own, [x_own] * (NC - 1), "ctx", NC)
    second = gather_rows(cfg, pack_b)
    up_send = call(functools.partial(send_upstream, cfg), [idx, ids, up_own], [((cfg.XC, D + EXTRA), bf)] * NE)
    ks = np.arange(E * CAP)
    to = (ks % cfg.XC) // CAP * (NE * CAP) + ks // cfg.XC * CAP + ks % CAP
    order = jnp.asarray(to.reshape(1, -1), jnp.int32)

    def to_experts(sent):
        got = spread(sent[0], sent[1:], "ep", NE)
        w = sent[0].shape[1]
        halves = call(
            functools.partial(arrange, cfg), [order, *got], [((E * CAP // HALVES, w), bf)] * HALVES,
            n_smem=0,
        )
        return [spread(h, [h] * (NC - 1), "ctx", NC) for h in halves]

    def from_experts(parts):
        got = []
        for half in parts:
            got += spread(half[0], half[1:], "ctx", NC)
        sent = call(functools.partial(gather_sum, cfg), [order, *got], [((cfg.XC, D), bf)] * NE, n_smem=0)
        return spread(sent[0], sent[1:], "ep", NE)

    ups = to_experts(up_send)
    nb = S // TILE
    x_all, q, k, v, hidden, att, lse, bias, w_all, gains = call(
        functools.partial(attn_forward, cfg), [idx, bucket, *first, *x_pieces],
        [((S, D), bf)] + [((hl, S, HD), bf)] * 3 + [((S, D), bf), ((S, CQ), bf), ((hl, S, 1), fl), ((hl, nb, TILE, TILE), fl),
         ((D, W1), bf), ((8, D), fl)],
        scratch=[pltpu.VMEM((hl, S, HD), fl)], flops=2e9,
    )
    atts = spread(att, [att] * (NC - 1), "ctx", NC)
    mixed, wo, router, *sent = call(
        functools.partial(middle, cfg), [idx, x_own, ids, gains, *atts, *second],
        [((B, D), fl), ((NC * CQ, D), bf), ((D, E), bf)] + [((cfg.XC, D), bf)] * NE,
        scratch=[pltpu.VMEM((D, D + E), bf)],
    )
    rows = to_experts(sent)
    backs, fwds, routes, grads = [], [], [], []
    for half in range(HALVES):
        got = experts(cfg, half, idx, rows[half], ups[half], expert_in, expert_out, router)
        backs.append(got[:NC])
        fwds.append(got[NC : 2 * NC])
        grads = expert_weights(cfg, half, *got[2 * NC : 2 * NC + 4], grads)
        routes.append(got[-1])
    grad_expert_in, grad_expert_out = grads
    back = from_experts(backs)
    mix, mix_half, gg = call(
        functools.partial(moe_back, cfg), [idx, ids, mixed, gains, up_own, *back],
        [((B, D), fl), ((B, D), bf), ((8, D), fl)],
    )
    fwd = from_experts(fwds)
    (block_output,) = call(functools.partial(finish_forward, cfg), [idx, ids, mixed, *fwd], [((B, D), fl)])
    gm = spread(mix_half, [mix_half] * (NC - 1), "ctx", NC)
    WC = 3 * CQ + CO + EXTRA
    mine, part, *gh = call(
        functools.partial(attn_backward, cfg),
        [idx, x_all, bucket, wo, q, k, v, hidden, lse, bias, w_all, gains, gg, *routes, *gm, *atts],
        [((D // 2, WC), bf)] * 2 + [((B, D), bf)] * NC,
        scratch=[
            pltpu.VMEM((hl, S, HD), bf),
            pltpu.VMEM((hl, S, HD), fl),
            pltpu.VMEM((hl, S, HD), fl),
            pltpu.VMEM((hl, S, HD), fl),
            pltpu.VMEM((S, S), bf),
            pltpu.VMEM((S, S), bf),
            pltpu.VMEM((hl, nb, TILE, TILE), fl),
            pltpu.VMEM((NC * CQ, WC), fl),
            pltpu.VMEM((S, D), bf),
            pltpu.VMEM((S, D), bf),
        ],
        flops=4e9,
    )
    theirs = permute(part, "ep", 1, NE)
    gh = spread(gh[0], gh[1:], "ctx", NC)
    pairs = call(functools.partial(add_pairs, cfg), [mine, theirs], [((R, WC), bf)] * (NE // 2), n_smem=0)
    pairs = [pairs[0]] + [permute(pairs[j], "ep", 2 * j, NE) for j in range(1, NE // 2)]
    (total,) = call(add_all, pairs, [((R, WC), bf)], n_smem=0)
    everyone = lax.all_gather(total, "ctx", axis=0, tiled=True)
    (input_grad,) = call(last_input, [x_own, gains, mix, *gh], [((B, D), fl)], n_smem=0)
    nbl = bias_table.shape[0]
    gq, gk, gv, go, grouter, gone, gtwo, gtable = call(
        functools.partial(last_weights, cfg), [everyone],
        [((R, D), fl)] * 4 + [((E, R), fl), ((1, R), fl), ((1, R), fl), ((nbl, cfg.H), fl)], n_smem=0,
    )
    return (
        block_output[None], input_grad[None], gq, gk, gv, go, grouter.T, gone[0], gtwo[0], gtable,
        grad_expert_in, grad_expert_out,
    )


def solution(mesh):
    two, three = P("ep", None), P("ep", "ctx", None)
    in_specs = (three, three, two, two, two, two, two, P("ep"), P("ep"), two, P(), three, P("ep", None, "ctx"), three)
    out_specs = (three, three, two, two, two, two, two, P("ep"), P("ep"), two, P("ep", None, "ctx"), three)
    return jax.shard_map(body, mesh=mesh, in_specs=in_specs, out_specs=out_specs, check_vma=False)
```

```python
import functools
import math

import jax
import jax.numpy as jnp
import numpy as np
from jax import lax
from jax.experimental import pallas as pl
from jax.experimental.pallas import tpu as pltpu
from jax.sharding import PartitionSpec as P


HD = 64
CAP = 6
TILE = 128
EXTRA = 128
HALVES = 2

EPS = 1e-06
SCALE = 0.125
INV_ROOT_TWO = 1.0 / math.sqrt(2.0)
INV_ROOT_TAU = 1.0 / math.sqrt(2.0 * math.pi)
NEG = -1e30

NN = (((1,), (0,)), ((), ()))
NT = (((1,), (1,)), ((), ()))
TN = (((0,), (0,)), ((), ()))


VMEM = pl.BlockSpec(memory_space=pltpu.VMEM)
SMEM = pl.BlockSpec(memory_space=pltpu.SMEM)


def f32(x):
    return x.astype(jnp.float32)


def b16(x):
    return x.astype(jnp.bfloat16)


def dot(a, b, dims=NN, precision=None):
    return lax.dot_general(a, b, dims, precision=precision, preferred_element_type=jnp.float32)


def iota(shape, axis):
    return lax.broadcasted_iota(jnp.int32, shape, axis)


def call(kernel, args, outs, scratch=(), flops=1e8, n_smem=1):
    size = sum(int(np.prod(a.shape)) * a.dtype.itemsize for a in args)
    size += sum(int(np.prod(s)) * jnp.dtype(d).itemsize for s, d in outs)
    return pl.pallas_call(
        kernel,
        out_shape=[jax.ShapeDtypeStruct(s, d) for s, d in outs],
        in_specs=[SMEM] * n_smem + [VMEM] * (len(args) - n_smem),
        out_specs=[VMEM] * len(outs),
        scratch_shapes=list(scratch),
        cost_estimate=pl.CostEstimate(flops=int(flops), bytes_accessed=size, transcendentals=0),
    )(*args)


def assemble(idx_ref, pieces, target, rows):
    if len(pieces) == 1:
        target[0 : pieces[0].shape[0], :] = pieces[0][...]
        return
    own = idx_ref[1]
    for order, piece in pieces:
        for n, off in enumerate(order):
            start = pl.multiple_of((own ^ off) * rows, rows)
            target[pl.ds(start, rows), :] = piece[n * rows : (n + 1) * rows, :]


def rms(x):
    inverse = lax.rsqrt(jnp.mean(x * x, axis=-1, keepdims=True) + EPS)
    return x * inverse, inverse


def table_select(buckets, width, rows, shards):
    per = buckets // shards
    b = iota((buckets, width), 0)
    shard = sum(((b >= per * s).astype(jnp.int32) for s in range(1, shards)), jnp.zeros_like(b))
    return iota((buckets, width), 1) == shard * rows + (b - shard * per)


def pack_weights(
    cfg, idx_ref, q_ref, k_ref, v_ref, o_ref, router_ref, one_ref, two_ref, table_ref, a_ref, b_ref, ext_ref
):
    R, CQ, D = cfg.rows, cfg.CQ, cfg.D
    width = cfg.NC * CQ
    shift = (cfg.NC - idx_ref[0]) * CQ
    for n, ref in enumerate((q_ref, k_ref, v_ref)):
        w = f32(ref[...])
        if width > D:
            w = jnp.concatenate([w, jnp.zeros((R, width - D), jnp.float32)], axis=1)
        a_ref[:, n * CQ : (n + 1) * CQ] = b16(pltpu.roll(w, shift, 1)[:, :CQ])
    ext_ref[...] = jnp.zeros_like(ext_ref)
    ext_ref[0 : table_ref.shape[0], 2 : 2 + cfg.H] = f32(table_ref[...])
    eye = (iota((R, R), 0) == iota((R, R), 1)).astype(jnp.float32)
    col_one = jnp.sum(eye * f32(one_ref[...]), axis=1, keepdims=True)
    col_two = jnp.sum(eye * f32(two_ref[...]), axis=1, keepdims=True)
    lane = iota((R, HD), 1)
    ext = ext_ref[:, :HD]
    ext = jnp.where(lane == 0, col_one, jnp.where(lane == 1, col_two, ext))
    a_ref[:, 3 * CQ :] = b16(ext)
    b_ref[:, :D] = o_ref[...]
    b_ref[:, D:] = b16(dot(b16(eye), router_ref[...], NT))


def place_blocks(cfg, idx_ref, pieces, target):
    for k, piece in enumerate(pieces):
        start = pl.multiple_of((idx_ref[0] ^ k) * cfg.B, cfg.B)
        target[pl.ds(start, cfg.B), :] = piece[...]


def attn_forward(cfg, idx_ref, bucket_ref, *refs):
    n_in = len(cfg.orders)
    pieces, refs = refs[:n_in], refs[n_in:]
    x_pieces, (x_ref, *refs) = refs[: cfg.NC], refs[cfg.NC :]
    place_blocks(cfg, idx_ref, x_pieces, x_ref)
    q_ref, k_ref, v_ref, hid_ref, att_ref, lse_ref, bias_ref, w_ref, gain_ref, ah_ref = refs
    assemble(idx_ref, cfg.pair(pieces), w_ref, cfg.rows)
    D, S, hl, CQ = cfg.D, cfg.S, cfg.hl, cfg.CQ
    extra = w_ref[:, 3 * CQ :]
    ew = extra.shape[1]
    pick = b16((iota((16, ew), 0) == iota((16, ew), 1)).astype(jnp.float32))
    gain_rows = dot(pick, extra, NT)
    gain_ref[...] = gain_rows[0:8]
    unit, _ = rms(f32(x_ref[...]))
    hidden = b16(unit * gain_rows[0:1])
    hid_ref[...] = hidden
    qkv = dot(hidden, w_ref[:, : 3 * CQ])
    for h in range(hl):
        q_ref[h] = b16(qkv[:, h * HD : (h + 1) * HD] * SCALE)
        k_ref[h] = b16(qkv[:, CQ + h * HD : CQ + (h + 1) * HD])
        v_ref[h] = b16(qkv[:, 2 * CQ + h * HD : 2 * CQ + (h + 1) * HD])
    table = dot(b16(table_select(cfg.NB, D, cfg.rows, cfg.NE).astype(jnp.float32)), extra)
    lane, col = iota((ew, 16), 0), iota((ew, 16), 1)
    head = idx_ref[0] * hl + col
    mine = (lane == 2 + head) & (col < hl) & (head < cfg.H)
    table = dot(b16(table), b16(mine.astype(jnp.float32)))
    hot = b16((iota((cfg.NB, S), 0) == bucket_ref[...]).astype(jnp.float32))
    offset_bias = dot(b16(table), hot, TN)
    nb = S // TILE
    keep = iota((TILE, TILE), 0) >= iota((TILE, TILE), 1)
    for h in range(hl):
        for k in range(nb):
            now = offset_bias[h : h + 1, k * TILE : (k + 1) * TILE]
            before = offset_bias[h : h + 1, (k - 1) * TILE : k * TILE] if k else now
            row = jnp.concatenate([now, before], axis=1)
            turned = pltpu.roll(
                jnp.broadcast_to(row, (TILE, 2 * TILE)), 0, 1, stride=1, stride_axis=0
            )
            tile = jnp.transpose(turned[:, :TILE])
            bias_ref[h, k] = jnp.where(keep, tile, NEG) if k == 0 else tile

    def one_head(h, carry):
        for ib in range(nb):
            n = (ib + 1) * TILE
            s = dot(q_ref[h, ib * TILE : n], k_ref[h, 0:n], NT)
            s = s + jnp.concatenate([bias_ref[h, ib - jb] for jb in range(ib + 1)], axis=1)
            peak = jnp.max(s, axis=1, keepdims=True)
            lse = peak + jnp.log(jnp.sum(jnp.exp(s - peak), axis=1, keepdims=True))
            lse_ref[h, ib * TILE : n] = lse
            ah_ref[h, ib * TILE : n] = dot(b16(jnp.exp(s - lse)), v_ref[h, 0:n])
        return carry

    lax.fori_loop(0, hl, one_head, 0)
    for h in range(hl):
        att_ref[:, h * HD : (h + 1) * HD] = b16(ah_ref[h])


def slots_of(ids, experts):
    n = ids.shape[0]
    first, second = ids[:, 0:1], ids[:, 1:2]
    e = iota((n, experts), 1)
    hot_a, hot_b = (e == first).astype(jnp.float32), (e == second).astype(jnp.float32)
    earlier = (iota((n, n), 0) > iota((n, n), 1)).astype(jnp.float32)
    count = dot(b16(earlier), b16(hot_a + hot_b))
    slot_a = first * CAP + jnp.sum(count * hot_a, axis=1, keepdims=True).astype(jnp.int32)
    slot_b = second * CAP + jnp.sum(count * hot_b, axis=1, keepdims=True).astype(jnp.int32)
    return slot_a, slot_b


def hot_slots(slot, start, width):
    return (slot == start + iota((slot.shape[0], width), 1)).astype(jnp.float32)


def send_upstream(cfg, idx_ref, ids_ref, up_ref, *outs):
    ids = ids_ref[...]
    slot_a, slot_b = slots_of(ids, cfg.E)
    n = cfg.XC
    other_a = b16(jnp.broadcast_to(f32(ids[:, 1:2]), (cfg.B, EXTRA)))
    other_b = b16(jnp.broadcast_to(f32(ids[:, 0:1]), (cfg.B, EXTRA)))
    for k in range(cfg.NE):
        start = (idx_ref[1] ^ k) * n
        hot_a, hot_b = hot_slots(slot_a, start, n), hot_slots(slot_b, start, n)
        outs[k][:, : cfg.D] = b16(dot(b16(hot_a + hot_b), up_ref[...], TN))
        outs[k][:, cfg.D :] = b16(dot(b16(hot_a), other_a, TN) + dot(b16(hot_b), other_b, TN))


def middle(cfg, idx_ref, x_ref, ids_ref, gain_ref, *refs):
    n_in = len(cfg.orders)
    atts, refs = refs[: cfg.NC], refs[cfg.NC :]
    pieces = refs[:n_in]
    mixed_ref, wo_ref, router_ref = refs[n_in : n_in + 3]
    outs = refs[n_in + 3 : n_in + 3 + cfg.NE]
    w_ref = refs[-1]
    assemble(idx_ref, cfg.pair(pieces), w_ref, cfg.rows)
    D, CQ = cfg.D, cfg.CQ
    wo_ref[0:D, :] = w_ref[:, :D]
    if cfg.NC * CQ > D:
        wo_ref[D:, :] = jnp.zeros((cfg.NC * CQ - D, D), jnp.bfloat16)
    router_ref[...] = w_ref[:, D : D + cfg.E]
    mixed = f32(x_ref[...])
    start = pl.multiple_of(idx_ref[0] * cfg.B, cfg.B)
    for k in range(cfg.NC):
        heads = pl.multiple_of((idx_ref[0] ^ k) * CQ, CQ)
        mixed = mixed + dot(atts[k][pl.ds(start, cfg.B), :], wo_ref[pl.ds(heads, CQ), :])
    mixed_ref[...] = mixed
    unit, _ = rms(mixed)
    hidden = b16(unit * gain_ref[1:2, :])
    slot_a, slot_b = slots_of(ids_ref[...], cfg.E)
    n = cfg.XC
    for k in range(cfg.NE):
        start = (idx_ref[1] ^ k) * n
        hot = hot_slots(slot_a, start, n) + hot_slots(slot_b, start, n)
        outs[k][...] = b16(dot(b16(hot), hidden, TN))


def arrange(cfg, cuts, order_ref, *refs):
    pieces, outs = refs[: cfg.NE], refs[cfg.NE :]
    rows = jnp.concatenate([p[...] for p in pieces], axis=0)
    total = rows.shape[0]
    part = total // HALVES
    for n in range(HALVES):
        hot = (iota((part, total), 0) + n * part == order_ref[...]).astype(jnp.float32)
        half = b16(dot(b16(hot), rows))
        for m, (lo, hi) in enumerate(cuts):
            outs[n * len(cuts) + m][...] = half[:, lo:hi]


def gather_sum(cfg, idx_ref, order_ref, *refs):
    ins, outs = refs[: HALVES * cfg.NC], refs[HALVES * cfg.NC :]
    halves = []
    for n in range(HALVES):
        group = ins[n * cfg.NC : (n + 1) * cfg.NC]
        total = f32(group[0][...])
        for piece in group[1:]:
            total = total + f32(piece[...])
        halves.append(b16(total))
    rows = jnp.concatenate(halves, axis=0)
    count = rows.shape[0]
    place = order_ref[0:1]
    if len(outs) == 1:
        place = order_ref[1:2] + (order_ref[2:3] ^ idx_ref[1]) * CAP
    hot = (iota((count, count), 0) == place).astype(jnp.float32)
    back = b16(dot(b16(hot), rows, TN))
    if len(outs) == 1:
        outs[0][...] = back
        return
    for k, out in enumerate(outs):
        out[...] = back[k * cfg.XC : (k + 1) * cfg.XC]


def collect(cfg, idx_ref, ids, pieces):
    slot_a, slot_b = slots_of(ids, cfg.E)
    total = None
    if len(pieces) == 1:
        hot = hot_slots(slot_a, 0, cfg.E * CAP) + hot_slots(slot_b, 0, cfg.E * CAP)
        return dot(b16(hot), pieces[0][...])
    for k, piece in enumerate(pieces):
        start = (idx_ref[1] ^ k) * cfg.XC
        hot = hot_slots(slot_a, start, cfg.XC) + hot_slots(slot_b, start, cfg.XC)
        term = dot(b16(hot), piece[...])
        total = term if total is None else total + term
    return total


def finish_forward(cfg, idx_ref, ids_ref, mixed_ref, *refs):
    refs[-1][...] = mixed_ref[...] + collect(cfg, idx_ref, ids_ref[...], refs[:-1])


def moe_back(cfg, idx_ref, ids_ref, mixed_ref, gain_ref, up_ref, *refs):
    pieces = refs[: cfg.NE]
    mix_ref, half_ref, gg_ref = refs[cfg.NE :]
    grad = collect(cfg, idx_ref, ids_ref[...], pieces)
    unit, inverse = rms(mixed_ref[...])
    gg_ref[...] = jnp.broadcast_to(jnp.sum(grad * unit, axis=0, keepdims=True), (8, cfg.D))
    scaled = grad * gain_ref[1:2, :]
    moved = inverse * (scaled - unit * jnp.mean(scaled * unit, axis=-1, keepdims=True))
    grad_mixed = f32(up_ref[...]) + moved
    mix_ref[...] = grad_mixed
    half_ref[...] = b16(grad_mixed)


def joined(refs):
    return jnp.concatenate([r[...] for r in refs], axis=0)


def join_parts(refs, parts):
    rows = [jnp.concatenate([r[...] for r in refs[n : n + parts]], axis=1) for n in range(0, len(refs), parts)]
    return jnp.concatenate(rows, axis=0)


def expert_kernel(cfg, first, parts, idx_ref, *refs):
    NC, D, E = cfg.NC, cfg.D, cfg.E
    rows_in, refs = refs[:NC], refs[NC:]
    ups_in, refs = refs[: parts * NC], refs[parts * NC :]
    win_ref, wout_ref, router_ref = refs[:3]
    outs = refs[3:]
    back, fwd = outs[:NC], outs[NC : 2 * NC]
    rows_out, up_out, act_out, pre_out, route_out = outs[2 * NC :]
    step = pl.program_id(0)
    own = idx_ref[1] * cfg.X + first + step
    rows = joined(rows_in)
    ups = join_parts(ups_in, parts)
    count = rows.shape[0]
    win, wout = win_ref[0], wout_ref[0]
    other = ups[:, D : D + 1].astype(jnp.float32).astype(jnp.int32)
    up = f32(ups[:, :D])
    lane = iota((count, E), 1)
    is_own = (lane == own).astype(jnp.float32)
    is_other = (lane == other).astype(jnp.float32)
    sign = is_own - is_other
    gap = jnp.sum(dot(rows, router_ref[...]) * sign, axis=1, keepdims=True)
    gate = jax.nn.sigmoid(gap)
    against = jax.nn.sigmoid(-gap)
    up_rows = b16(gate * up)
    preact = dot(rows, win)
    cdf = 0.5 * (1.0 + lax.erf(preact * INV_ROOT_TWO))
    slope = cdf + preact * jnp.exp(-0.5 * preact * preact) * INV_ROOT_TAU
    active = b16(preact * cdf)
    part = dot(active, wout)
    grad_pre = b16(dot(up_rows, wout, NT) * slope)
    weight = gate * against * jnp.sum(up * part, axis=1, keepdims=True)
    coef = weight * sign
    high = b16(coef)
    low = b16(coef - f32(high))
    route_ref = router_ref[...]
    both = jnp.concatenate([f32(high), f32(low)], axis=1).astype(jnp.bfloat16)
    wide = jnp.concatenate([f32(route_ref), f32(route_ref)], axis=1).astype(jnp.bfloat16)
    back_rows = dot(grad_pre, win, NT) + dot(both, wide, NT)
    route = dot(rows, both, TN)

    @pl.when(step == 0)
    def _():
        route_out[...] = route

    @pl.when(step > 0)
    def _():
        route_out[...] += route

    fwd_rows = b16(gate * part)
    back_rows = b16(back_rows)
    each = count // NC
    for c in range(NC):
        back[c][...] = back_rows[c * each : (c + 1) * each]
        fwd[c][...] = fwd_rows[c * each : (c + 1) * each]
    rows_out[0] = rows
    up_out[0] = up_rows
    act_out[0] = active
    pre_out[0] = grad_pre


def experts(cfg, half, cuts, idx, rows, ups, w_in, w_out, router):
    NC, D, FL = cfg.NC, cfg.D, w_in.shape[2]
    steps = cfg.X // HALVES
    first = half * steps
    each = cfg.NE * CAP
    count = NC * each
    fixed = lambda shape: pl.BlockSpec(shape, lambda s: (0,) * len(shape))
    row = lambda w: pl.BlockSpec((each, w), lambda s: (s, 0))
    per = lambda a, b: pl.BlockSpec((1, a, b), lambda s: (first + s, 0, 0))
    here = lambda a, b: pl.BlockSpec((1, a, b), lambda s: (s, 0, 0))
    saved = [((steps, count, w), jnp.bfloat16) for w in (D, D, FL, FL)]
    outs = [((steps * each, D), jnp.bfloat16)] * (2 * NC) + saved + [((D, 2 * cfg.E), jnp.float32)]
    in_specs = [SMEM] + [row(D)] * NC + [row(hi - lo) for lo, hi in cuts] * NC
    in_specs += [per(D, FL), per(FL, D), fixed((D, cfg.E))]
    out_specs = [row(D)] * (2 * NC) + [here(count, w) for w in (D, D, FL, FL)]
    out_specs += [fixed((D, 2 * cfg.E))]
    return pl.pallas_call(
        functools.partial(expert_kernel, cfg, first, len(cuts)),
        grid=(steps,),
        out_shape=[jax.ShapeDtypeStruct(s, d) for s, d in outs],
        in_specs=in_specs,
        out_specs=out_specs,
        cost_estimate=pl.CostEstimate(
            flops=steps * 4 * 2 * count * D * FL, bytes_accessed=steps * 4 * D * FL, transcendentals=0
        ),
    )(idx, *rows, *ups, w_in, w_out, router)


def expert_weights_kernel(rows_ref, up_ref, act_ref, pre_ref, *refs):
    gin_ref, gout_ref = refs[-2:]
    gin_ref[0] = dot(rows_ref[0], pre_ref[0], TN)
    gout_ref[0] = dot(act_ref[0], up_ref[0], TN)


def expert_weights(cfg, half, rows, up, act, pre, earlier):
    steps, count, D = rows.shape
    FL = act.shape[2]
    here = lambda a, b: pl.BlockSpec((1, a, b), lambda s: (s, 0, 0))
    per = lambda a, b: pl.BlockSpec((1, a, b), lambda s: (half * steps + s, 0, 0))
    return pl.pallas_call(
        expert_weights_kernel,
        grid=(steps,),
        out_shape=[
            jax.ShapeDtypeStruct((cfg.X, D, FL), jnp.float32),
            jax.ShapeDtypeStruct((cfg.X, FL, D), jnp.float32),
        ],
        in_specs=[here(count, D), here(count, D), here(count, FL), here(count, FL)]
        + [pl.BlockSpec(memory_space=pl.ANY)] * len(earlier),
        out_specs=[per(D, FL), per(FL, D)],
        input_output_aliases={4 + n: n for n in range(len(earlier))},
        cost_estimate=pl.CostEstimate(
            flops=steps * 4 * count * D * FL, bytes_accessed=steps * 8 * D * FL, transcendentals=0
        ),
    )(rows, up, act, pre, *earlier)


def attn_backward(
    cfg, idx_ref, x_ref, bucket_ref, wo_ref, q_ref, k_ref, v_ref, hid_ref, lse_ref,
    bias_ref, w_ref, gain_ref, gg_ref, *refs,
):
    NC = cfg.NC
    routes, refs = refs[:HALVES], refs[HALVES:]
    gm_in, atts, refs = refs[:NC], refs[NC : 2 * NC], refs[2 * NC :]
    mine_ref, part_ref, *gh_out = refs[: 2 + NC]
    da_ref, dq_ref, dk_ref, dv_ref, p_ref, ds_ref, acc_ref, dw_ref, gm_ref, gh_ref = refs[2 + NC :]
    D, S, hl, CQ, CO, B = cfg.D, cfg.S, cfg.hl, cfg.CQ, cfg.CO, cfg.B
    nb = S // TILE
    c = idx_ref[0]
    place_blocks(cfg, idx_ref, gm_in, gm_ref)
    gm = gm_ref[...]
    own = pl.multiple_of(c * CQ, CQ)
    grad_att = b16(dot(gm, wo_ref[pl.ds(own, CQ), :], NT))
    for h in range(hl):
        da_ref[h] = grad_att[:, h * HD : (h + 1) * HD]
    prod = f32(grad_att) * f32(atts[0][...])
    deltas = [jnp.sum(prod[:, h * HD : (h + 1) * HD], axis=1, keepdims=True) for h in range(hl)]
    acc_ref[...] = jnp.zeros_like(acc_ref)
    for ib in range(nb):
        if ib + 1 < nb:
            zero = jnp.zeros((TILE, S - (ib + 1) * TILE), jnp.bfloat16)
            p_ref[ib * TILE : (ib + 1) * TILE, (ib + 1) * TILE :] = zero
            ds_ref[ib * TILE : (ib + 1) * TILE, (ib + 1) * TILE :] = zero
    for h in range(hl):
        for ib in range(nb):
            lo, n = ib * TILE, (ib + 1) * TILE
            s = dot(q_ref[h, lo:n], k_ref[h, 0:n], NT)
            s = s + jnp.concatenate([bias_ref[h, ib - jb] for jb in range(ib + 1)], axis=1)
            prob = jnp.exp(s - lse_ref[h, lo:n])
            grad_p = dot(da_ref[h, lo:n], v_ref[h, 0:n], NT)
            grad_s = prob * (grad_p - deltas[h][lo:n])
            p_ref[lo:n, 0:n] = b16(prob)
            half = b16(grad_s)
            ds_ref[lo:n, 0:n] = half
            dq_ref[h, lo:n] = dot(half, k_ref[h, 0:n]) * SCALE
            for jb in range(ib + 1):
                acc_ref[h, ib - jb] += grad_s[:, jb * TILE : (jb + 1) * TILE]
        dk_ref[h] = dot(ds_ref[...], q_ref[h], TN)
        dv_ref[h] = dot(p_ref[...], da_ref[h], TN)
    per_offset = []
    zero_tile = jnp.zeros((TILE, TILE), jnp.float32)
    sub = iota((8, 2 * TILE), 0)
    for h in range(hl):
        rows = []
        for k in range(nb):
            wide = jnp.concatenate([jnp.transpose(acc_ref[h, k]), zero_tile], axis=1)
            total = wide[0:8]
            for g in range(1, TILE // 8):
                total = total + pltpu.roll(wide[g * 8 : (g + 1) * 8], 2 * TILE - 8 * g, 1)
            for bit in (1, 2, 4):
                total = jnp.where((sub & bit) != 0, pltpu.roll(total, 2 * TILE - bit, 1), total)
            rows.append(jnp.sum(total, axis=0, keepdims=True))
        spans = []
        for k in range(nb):
            span = rows[k][:, :TILE]
            if k + 1 < nb:
                span = span + rows[k + 1][:, TILE:]
            spans.append(span)
        per_offset.append(jnp.concatenate(spans, axis=1))
    per_offset.append(jnp.zeros((8 - hl, S), jnp.float32))
    per_offset = jnp.concatenate(per_offset, axis=0)
    hot = (iota((cfg.NB, S), 0) == bucket_ref[...]).astype(jnp.float32)
    table = dot(per_offset, hot, NT, lax.Precision.HIGHEST)
    place = table_select(cfg.NB, D, cfg.rows, cfg.NE).astype(jnp.float32)
    table_rows = dot(table, place, NN, lax.Precision.HIGHEST)
    grads = jnp.concatenate(
        [dq_ref[h] for h in range(hl)] + [dk_ref[h] for h in range(hl)] + [dv_ref[h] for h in range(hl)],
        axis=1,
    )
    grads = b16(grads)
    dw_ref[0:D, : 3 * CQ] = dot(hid_ref[...], grads, TN)
    sel = b16((iota((D, CO), 0) == c * CO + iota((D, CO), 1)).astype(jnp.float32))
    gm_cols = b16(dot(gm, sel))
    for k in range(NC):
        heads = pl.multiple_of((c ^ k) * CQ, CQ)
        dw_ref[pl.ds(heads, CQ), 3 * CQ : 3 * CQ + CO] = dot(atts[k][...], gm_cols, TN)
    gh = dot(grads, w_ref[:, : 3 * CQ], NT)
    gh_ref[...] = b16(gh)
    for k, out in enumerate(gh_out):
        out[...] = gh_ref[pl.ds(pl.multiple_of((c ^ k) * B, B), B), :]
    unit, _ = rms(f32(x_ref[...]))
    gain_one = jnp.sum(gh * unit, axis=0, keepdims=True)
    E = cfg.E
    stack = jnp.concatenate(
        [
            jnp.zeros((E, D), jnp.float32),
            gain_one,
            gg_ref[0:1, :],
            table_rows[0:hl],
            jnp.zeros((EXTRA - E - 2 - hl, D), jnp.float32),
        ],
        axis=0,
    )
    extra = jnp.transpose(stack)
    route = routes[0][...]
    for r in routes[1:]:
        route = route + r[...]
    route = route[:, :E] + route[:, E:]
    extra = extra + jnp.concatenate([route, jnp.zeros((D, EXTRA - E), jnp.float32)], axis=1)
    dw_ref[0:D, 3 * CQ + CO :] = extra
    me = idx_ref[1]
    R = cfg.rows
    for j in range(cfg.NE // 2):
        a = pl.multiple_of((me ^ (2 * j)) * R, R)
        b = pl.multiple_of((me ^ (2 * j + 1)) * R, R)
        mine_ref[j * R : (j + 1) * R, :] = b16(dw_ref[pl.ds(a, R), :])
        part_ref[j * R : (j + 1) * R, :] = b16(dw_ref[pl.ds(b, R), :])


def add_pairs(cfg, a_ref, b_ref, *outs):
    R = cfg.rows
    for j, out in enumerate(outs):
        out[...] = b16(f32(a_ref[j * R : (j + 1) * R]) + f32(b_ref[j * R : (j + 1) * R]))


def add_all(*refs):
    total = f32(refs[0][...])
    for r in refs[1:-1]:
        total = total + f32(r[...])
    refs[-1][...] = b16(total)


def last_input(x_ref, gain_ref, mix_ref, *refs):
    out_ref = refs[-1]
    total = f32(refs[0][...])
    for ref in refs[1:-1]:
        total = total + f32(ref[...])
    unit, inverse = rms(f32(x_ref[...]))
    scaled = total * gain_ref[0:1, :]
    moved = inverse * (scaled - unit * jnp.mean(scaled * unit, axis=-1, keepdims=True))
    out_ref[...] = mix_ref[...] + moved


def last_weights(cfg, idx_ref, *refs):
    ins, (q_ref, k_ref, v_ref, o_ref, router_ref, one_ref, two_ref, table_ref, all_ref) = refs[: cfg.NC], refs[cfg.NC :]
    R, CQ, CO, D, hl, E = cfg.rows, cfg.CQ, cfg.CO, cfg.D, cfg.hl, cfg.E
    for k, piece in enumerate(ins):
        all_ref[idx_ref[0] ^ k] = f32(piece[...])
    pieces = [all_ref[n] for n in range(cfg.NC)]
    for t, ref in enumerate((q_ref, k_ref, v_ref)):
        full = jnp.concatenate([p[:, t * CQ : (t + 1) * CQ] for p in pieces], axis=1)
        ref[...] = full[:, :D]
    o_ref[...] = jnp.concatenate([p[:, 3 * CQ : 3 * CQ + CO] for p in pieces], axis=1)
    base = 3 * CQ + CO
    extra = pieces[0][:, base:]
    for p in pieces[1:]:
        extra = extra + p[:, base:]
    router_ref[...] = jnp.transpose(extra)[:E]
    eye = (iota((R, R), 0) == iota((R, R), 1)).astype(jnp.float32)
    one_ref[...] = jnp.sum(eye * extra[:, E : E + 1], axis=0, keepdims=True)
    two_ref[...] = jnp.sum(eye * extra[:, E + 1 : E + 2], axis=0, keepdims=True)
    table = jnp.concatenate([p[:, base + E + 2 : base + E + 2 + hl] for p in pieces], axis=1)
    table_ref[...] = table[: cfg.NB // cfg.NE, : cfg.H]


class Config:
    def pair(self, pieces):
        if len(pieces) == 1:
            return list(pieces)
        return list(zip(self.orders, pieces, strict=True))


def permute(x, axis, k, n):
    return lax.ppermute(x, axis, [(i, i ^ k) for i in range(n)])


def spread(first, rest, axis, n):
    return [first] + [permute(x, axis, k, n) for k, x in zip(range(1, n), rest, strict=True)]


def two_steps(parts):
    got = []
    for part, (near, via) in zip(parts, ((1, 2), (2, 1)), strict=True):
        one, two = permute(part, "ctx", near, 4), permute(part, "ctx", via, 4)
        far = permute(one, "ctx", via, 4)
        got.append([part, one, two, far] if near == 1 else [part, two, one, far])
    return got


def gather_rows(cfg, x):
    if len(cfg.orders) == 1:
        return [lax.all_gather(x, "ep", axis=0, tiled=True)]
    got = [x] + [permute(x, "ep", 2 * j, cfg.NE) for j in range(1, cfg.NE // 2)]
    return got + [permute(g, "ep", 1, cfg.NE) for g in got]


def body(
    block_input, out_grad, w_query, w_key, w_value, w_output, w_router, attn_gain, moe_gain,
    bias_table, rel_bucket, expert_ids, expert_in, expert_out,
):
    cfg = Config()
    NC, NE = lax.axis_size("ctx"), lax.axis_size("ep")
    B, D = block_input.shape[1:]
    S = rel_bucket.shape[0]
    cfg.NC, cfg.NE, cfg.B, cfg.D, cfg.S = NC, NE, B, D, S
    cfg.H = D // HD
    cfg.hl = -(-cfg.H // NC)
    cfg.CQ = CQ = cfg.hl * HD
    cfg.CO = CO = D // NC
    cfg.rows = R = D // NE
    cfg.X = X = expert_in.shape[0]
    cfg.E = E = X * NE
    cfg.XC = X * CAP
    cfg.NB = bias_table.shape[0] * NE
    hl = cfg.hl
    if R % 16 == 0:
        cfg.orders = [(2 * j,) for j in range(NE // 2)] + [(2 * j + 1,) for j in range(NE // 2)]
    else:
        cfg.orders = [None]
    bf, fl = jnp.bfloat16, jnp.float32
    c, e = lax.axis_index("ctx"), lax.axis_index("ep")
    idx = jnp.stack([c, e]).astype(jnp.int32)
    x_own, up_own, ids = block_input[0], out_grad[0], expert_ids[0]
    bucket = rel_bucket.reshape(1, S)

    W1 = 3 * CQ + HD
    pack_a, pack_b = call(
        functools.partial(pack_weights, cfg),
        [idx, w_query, w_key, w_value, w_output, w_router.T, attn_gain[None], moe_gain[None], bias_table],
        [((R, W1), bf), ((R, D + E), bf)], scratch=[pltpu.VMEM((R, TILE), fl)],
    )
    first = gather_rows(cfg, pack_a)
    x_pieces = spread(x_own, [x_own] * (NC - 1), "ctx", NC)
    second = gather_rows(cfg, pack_b)
    up_send = call(functools.partial(send_upstream, cfg), [idx, ids, up_own], [((cfg.XC, D + EXTRA), bf)] * NE)
    ks = np.arange(E * CAP)
    to = (ks % cfg.XC) // CAP * (NE * CAP) + ks // cfg.XC * CAP + ks % CAP
    order = jnp.asarray(to.reshape(1, -1), jnp.int32)
    source = ks // cfg.XC
    orders = jnp.asarray(np.stack([to, to - source * CAP, source]), jnp.int32)

    def to_experts(sent, cuts):
        got = spread(sent[0], sent[1:], "ep", NE)
        parts = call(
            functools.partial(arrange, cfg, cuts), [order, *got],
            [((E * CAP // HALVES, hi - lo), bf) for lo, hi in cuts] * HALVES, n_smem=0,
        )
        out = []
        for n in range(HALVES):
            here = parts[n * len(cuts) : (n + 1) * len(cuts)]
            if len(cuts) == 2 and NC == 4:
                got = two_steps(here)
            else:
                got = [spread(h, [h] * (NC - 1), "ctx", NC) for h in here]
            out.append([piece[k] for k in range(NC) for piece in got])
        return out

    def from_experts(parts, whole):
        got = []
        for half in parts:
            got += spread(half[0], half[1:], "ctx", NC)
        sent = call(
            functools.partial(gather_sum, cfg), [idx, orders, *got],
            [((E * CAP, D), bf)] if whole else [((cfg.XC, D), bf)] * NE,
        )
        if whole:
            return [lax.all_to_all(sent[0], "ep", split_axis=0, concat_axis=0, tiled=True)]
        return spread(sent[0], sent[1:], "ep", NE)

    W2 = D + EXTRA
    cut = (D // 2 + EXTRA - 1) // EXTRA * EXTRA
    cuts = ((0, cut), (cut, W2))
    ups = to_experts(up_send, cuts)
    nb = S // TILE
    x_all, q, k, v, hidden, att, lse, bias, w_all, gains = call(
        functools.partial(attn_forward, cfg), [idx, bucket, *first, *x_pieces],
        [((S, D), bf)] + [((hl, S, HD), bf)] * 3 + [((S, D), bf), ((S, CQ), bf), ((hl, S, 1), fl), ((hl, nb, TILE, TILE), fl),
         ((D, W1), bf), ((8, D), fl)],
        scratch=[pltpu.VMEM((hl, S, HD), fl)], flops=2e9,
    )
    atts = spread(att, [att] * (NC - 1), "ctx", NC)
    mixed, wo, router, *sent = call(
        functools.partial(middle, cfg), [idx, x_own, ids, gains, *atts, *second],
        [((B, D), fl), ((NC * CQ, D), bf), ((D, E), bf)] + [((cfg.XC, D), bf)] * NE,
        scratch=[pltpu.VMEM((D, D + E), bf)],
    )
    rows = to_experts(sent, ((0, D),))
    backs, fwds, routes, grads = [], [], [], []
    for half in range(HALVES):
        got = experts(cfg, half, cuts, idx, rows[half], ups[half], expert_in, expert_out, router)
        backs.append(got[:NC])
        fwds.append(got[NC : 2 * NC])
        grads = expert_weights(cfg, half, *got[2 * NC : 2 * NC + 4], grads)
        routes.append(got[-1])
    grad_expert_in, grad_expert_out = grads
    back = from_experts(backs, False)
    mix, mix_half, gg = call(
        functools.partial(moe_back, cfg), [idx, ids, mixed, gains, up_own, *back],
        [((B, D), fl), ((B, D), bf), ((8, D), fl)],
    )
    fwd = from_experts(fwds, True)
    (block_output,) = call(functools.partial(finish_forward, cfg), [idx, ids, mixed, *fwd], [((B, D), fl)])
    gm = spread(mix_half, [mix_half] * (NC - 1), "ctx", NC)
    WC = 3 * CQ + CO + EXTRA
    mine, part, *gh = call(
        functools.partial(attn_backward, cfg),
        [idx, x_all, bucket, wo, q, k, v, hidden, lse, bias, w_all, gains, gg, *routes, *gm, *atts],
        [((D // 2, WC), bf)] * 2 + [((B, D), bf)] * NC,
        scratch=[
            pltpu.VMEM((hl, S, HD), bf),
            pltpu.VMEM((hl, S, HD), fl),
            pltpu.VMEM((hl, S, HD), fl),
            pltpu.VMEM((hl, S, HD), fl),
            pltpu.VMEM((S, S), bf),
            pltpu.VMEM((S, S), bf),
            pltpu.VMEM((hl, nb, TILE, TILE), fl),
            pltpu.VMEM((NC * CQ, WC), fl),
            pltpu.VMEM((S, D), bf),
            pltpu.VMEM((S, D), bf),
        ],
        flops=4e9,
    )
    theirs = permute(part, "ep", 1, NE)
    gh = spread(gh[0], gh[1:], "ctx", NC)
    pairs = call(functools.partial(add_pairs, cfg), [mine, theirs], [((R, WC), bf)] * (NE // 2), n_smem=0)
    pairs = [pairs[0]] + [permute(pairs[j], "ep", 2 * j, NE) for j in range(1, NE // 2)]
    (total,) = call(add_all, pairs, [((R, WC), bf)], n_smem=0)
    everyone = spread(total, [total] * (NC - 1), "ctx", NC)
    (input_grad,) = call(last_input, [x_own, gains, mix, *gh], [((B, D), fl)], n_smem=0)
    nbl = bias_table.shape[0]
    gq, gk, gv, go, grouter, gone, gtwo, gtable = call(
        functools.partial(last_weights, cfg), [idx, *everyone],
        [((R, D), fl)] * 4 + [((E, R), fl), ((1, R), fl), ((1, R), fl), ((nbl, cfg.H), fl)],
        scratch=[pltpu.VMEM((NC, R, WC), fl)],
    )
    return (
        block_output[None], input_grad[None], gq, gk, gv, go, grouter.T, gone[0], gtwo[0], gtable,
        grad_expert_in, grad_expert_out,
    )


def solution(mesh):
    two, three = P("ep", None), P("ep", "ctx", None)
    in_specs = (three, three, two, two, two, two, two, P("ep"), P("ep"), two, P(), three, P("ep", None, "ctx"), three)
    out_specs = (three, three, two, two, two, two, two, P("ep"), P("ep"), two, P("ep", None, "ctx"), three)
    return jax.shard_map(body, mesh=mesh, in_specs=in_specs, out_specs=out_specs, check_vma=False)
```

```python
import functools
import math

import jax
import jax.numpy as jnp
import numpy as np
from jax import lax
from jax.experimental import pallas as pl
from jax.experimental.pallas import tpu as pltpu
from jax.sharding import PartitionSpec as P


HD = 64
CAP = 6
TILE = 128
EXTRA = 128
HALVES = 2

EPS = 1e-06
SCALE = 0.125
INV_ROOT_TWO = 1.0 / math.sqrt(2.0)
INV_ROOT_TAU = 1.0 / math.sqrt(2.0 * math.pi)
NEG = -1e30

NN = (((1,), (0,)), ((), ()))
NT = (((1,), (1,)), ((), ()))
TN = (((0,), (0,)), ((), ()))


VMEM = pl.BlockSpec(memory_space=pltpu.VMEM)
SMEM = pl.BlockSpec(memory_space=pltpu.SMEM)


def f32(x):
    return x.astype(jnp.float32)


def b16(x):
    return x.astype(jnp.bfloat16)


def dot(a, b, dims=NN, precision=None):
    return lax.dot_general(a, b, dims, precision=precision, preferred_element_type=jnp.float32)


def iota(shape, axis):
    return lax.broadcasted_iota(jnp.int32, shape, axis)


def call(kernel, args, outs, scratch=(), flops=1e8, n_smem=1):
    size = sum(int(np.prod(a.shape)) * a.dtype.itemsize for a in args)
    size += sum(int(np.prod(s)) * jnp.dtype(d).itemsize for s, d in outs)
    return pl.pallas_call(
        kernel,
        out_shape=[jax.ShapeDtypeStruct(s, d) for s, d in outs],
        in_specs=[SMEM] * n_smem + [VMEM] * (len(args) - n_smem),
        out_specs=[VMEM] * len(outs),
        scratch_shapes=list(scratch),
        cost_estimate=pl.CostEstimate(flops=int(flops), bytes_accessed=size, transcendentals=0),
    )(*args)


def assemble(idx_ref, pieces, target, rows):
    if len(pieces) == 1:
        target[0 : pieces[0].shape[0], :] = pieces[0][...]
        return
    own = idx_ref[1]
    for order, piece in pieces:
        for n, off in enumerate(order):
            start = pl.multiple_of((own ^ off) * rows, rows)
            target[pl.ds(start, rows), :] = piece[n * rows : (n + 1) * rows, :]


def rms(x):
    inverse = lax.rsqrt(jnp.mean(x * x, axis=-1, keepdims=True) + EPS)
    return x * inverse, inverse


def table_select(buckets, width, rows, shards):
    per = buckets // shards
    b = iota((buckets, width), 0)
    shard = sum(((b >= per * s).astype(jnp.int32) for s in range(1, shards)), jnp.zeros_like(b))
    return iota((buckets, width), 1) == shard * rows + (b - shard * per)


def pack_weights(
    cfg, idx_ref, q_ref, k_ref, v_ref, o_ref, router_ref, one_ref, two_ref, table_ref, a_ref, b_ref, ext_ref
):
    R, CQ, D = cfg.rows, cfg.CQ, cfg.D
    width = cfg.NC * CQ
    shift = (cfg.NC - idx_ref[0]) * CQ
    for n, ref in enumerate((q_ref, k_ref, v_ref)):
        w = f32(ref[...])
        if width > D:
            w = jnp.concatenate([w, jnp.zeros((R, width - D), jnp.float32)], axis=1)
        a_ref[:, n * CQ : (n + 1) * CQ] = b16(pltpu.roll(w, shift, 1)[:, :CQ])
    ext_ref[...] = jnp.zeros_like(ext_ref)
    ext_ref[0 : table_ref.shape[0], 2 : 2 + cfg.H] = f32(table_ref[...])
    eye = (iota((R, R), 0) == iota((R, R), 1)).astype(jnp.float32)
    col_one = jnp.sum(eye * f32(one_ref[...]), axis=1, keepdims=True)
    col_two = jnp.sum(eye * f32(two_ref[...]), axis=1, keepdims=True)
    lane = iota((R, HD), 1)
    ext = ext_ref[:, :HD]
    ext = jnp.where(lane == 0, col_one, jnp.where(lane == 1, col_two, ext))
    a_ref[:, 3 * CQ :] = b16(ext)
    b_ref[:, :D] = o_ref[...]
    b_ref[:, D:] = b16(dot(b16(eye), router_ref[...], NT))


def place_blocks(cfg, idx_ref, pieces, target):
    for k, piece in enumerate(pieces):
        start = pl.multiple_of((idx_ref[0] ^ k) * cfg.B, cfg.B)
        target[pl.ds(start, cfg.B), :] = piece[...]


def attn_forward(cfg, idx_ref, bucket_ref, *refs):
    n_in = len(cfg.orders)
    pieces, refs = refs[:n_in], refs[n_in:]
    x_pieces, (x_ref, *refs) = refs[: cfg.NC], refs[cfg.NC :]
    place_blocks(cfg, idx_ref, x_pieces, x_ref)
    q_ref, k_ref, v_ref, hid_ref, att_ref, lse_ref, bias_ref, w_ref, gain_ref, ah_ref = refs
    assemble(idx_ref, cfg.pair(pieces), w_ref, cfg.rows)
    D, S, hl, CQ = cfg.D, cfg.S, cfg.hl, cfg.CQ
    extra = w_ref[:, 3 * CQ :]
    ew = extra.shape[1]
    pick = b16((iota((16, ew), 0) == iota((16, ew), 1)).astype(jnp.float32))
    gain_rows = dot(pick, extra, NT)
    gain_ref[...] = gain_rows[0:8]
    unit, _ = rms(f32(x_ref[...]))
    hidden = b16(unit * gain_rows[0:1])
    hid_ref[...] = hidden
    qkv = dot(hidden, w_ref[:, : 3 * CQ])
    for h in range(hl):
        q_ref[h] = b16(qkv[:, h * HD : (h + 1) * HD] * SCALE)
        k_ref[h] = b16(qkv[:, CQ + h * HD : CQ + (h + 1) * HD])
        v_ref[h] = b16(qkv[:, 2 * CQ + h * HD : 2 * CQ + (h + 1) * HD])
    table = dot(b16(table_select(cfg.NB, D, cfg.rows, cfg.NE).astype(jnp.float32)), extra)
    lane, col = iota((ew, 16), 0), iota((ew, 16), 1)
    head = idx_ref[0] * hl + col
    mine = (lane == 2 + head) & (col < hl) & (head < cfg.H)
    table = dot(b16(table), b16(mine.astype(jnp.float32)))
    hot = b16((iota((cfg.NB, S), 0) == bucket_ref[...]).astype(jnp.float32))
    offset_bias = dot(b16(table), hot, TN)
    nb = S // TILE
    keep = iota((TILE, TILE), 0) >= iota((TILE, TILE), 1)
    for h in range(hl):
        for k in range(nb):
            now = offset_bias[h : h + 1, k * TILE : (k + 1) * TILE]
            before = offset_bias[h : h + 1, (k - 1) * TILE : k * TILE] if k else now
            row = jnp.concatenate([now, before], axis=1)
            turned = pltpu.roll(
                jnp.broadcast_to(row, (TILE, 2 * TILE)), 0, 1, stride=1, stride_axis=0
            )
            tile = jnp.transpose(turned[:, :TILE])
            bias_ref[h, k] = jnp.where(keep, tile, NEG) if k == 0 else tile

    def one_head(h, carry):
        for ib in range(nb):
            n = (ib + 1) * TILE
            s = dot(q_ref[h, ib * TILE : n], k_ref[h, 0:n], NT)
            s = s + jnp.concatenate([bias_ref[h, ib - jb] for jb in range(ib + 1)], axis=1)
            peak = jnp.max(s, axis=1, keepdims=True)
            lse = peak + jnp.log(jnp.sum(jnp.exp(s - peak), axis=1, keepdims=True))
            lse_ref[h, ib * TILE : n] = lse
            ah_ref[h, ib * TILE : n] = dot(b16(jnp.exp(s - lse)), v_ref[h, 0:n])
        return carry

    lax.fori_loop(0, hl, one_head, 0)
    for h in range(hl):
        att_ref[:, h * HD : (h + 1) * HD] = b16(ah_ref[h])


def slots_of(ids, experts):
    n = ids.shape[0]
    first, second = ids[:, 0:1], ids[:, 1:2]
    e = iota((n, experts), 1)
    hot_a, hot_b = (e == first).astype(jnp.float32), (e == second).astype(jnp.float32)
    earlier = (iota((n, n), 0) > iota((n, n), 1)).astype(jnp.float32)
    count = dot(b16(earlier), b16(hot_a + hot_b))
    slot_a = first * CAP + jnp.sum(count * hot_a, axis=1, keepdims=True).astype(jnp.int32)
    slot_b = second * CAP + jnp.sum(count * hot_b, axis=1, keepdims=True).astype(jnp.int32)
    return slot_a, slot_b


def hot_slots(slot, start, width):
    return (slot == start + iota((slot.shape[0], width), 1)).astype(jnp.float32)


def send_upstream(cfg, idx_ref, ids_ref, up_ref, *outs):
    ids = ids_ref[...]
    slot_a, slot_b = slots_of(ids, cfg.E)
    n = cfg.XC
    other_a = b16(jnp.broadcast_to(f32(ids[:, 1:2]), (cfg.B, EXTRA)))
    other_b = b16(jnp.broadcast_to(f32(ids[:, 0:1]), (cfg.B, EXTRA)))
    for k in range(cfg.NE):
        start = (idx_ref[1] ^ k) * n
        hot_a, hot_b = hot_slots(slot_a, start, n), hot_slots(slot_b, start, n)
        outs[k][:, : cfg.D] = b16(dot(b16(hot_a + hot_b), up_ref[...], TN))
        outs[k][:, cfg.D :] = b16(dot(b16(hot_a), other_a, TN) + dot(b16(hot_b), other_b, TN))


def middle(cfg, idx_ref, x_ref, ids_ref, gain_ref, *refs):
    n_in = len(cfg.orders)
    atts, refs = refs[: cfg.NC], refs[cfg.NC :]
    pieces = refs[:n_in]
    mixed_ref, wo_ref, router_ref = refs[n_in : n_in + 3]
    outs = refs[n_in + 3 : n_in + 3 + cfg.NE]
    w_ref = refs[-1]
    assemble(idx_ref, cfg.pair(pieces), w_ref, cfg.rows)
    D, CQ = cfg.D, cfg.CQ
    wo_ref[0:D, :] = w_ref[:, :D]
    if cfg.NC * CQ > D:
        wo_ref[D:, :] = jnp.zeros((cfg.NC * CQ - D, D), jnp.bfloat16)
    router_ref[...] = w_ref[:, D : D + cfg.E]
    mixed = f32(x_ref[...])
    start = pl.multiple_of(idx_ref[0] * cfg.B, cfg.B)
    for k in range(cfg.NC):
        heads = pl.multiple_of((idx_ref[0] ^ k) * CQ, CQ)
        mixed = mixed + dot(atts[k][pl.ds(start, cfg.B), :], wo_ref[pl.ds(heads, CQ), :])
    mixed_ref[...] = mixed
    unit, _ = rms(mixed)
    hidden = b16(unit * gain_ref[1:2, :])
    slot_a, slot_b = slots_of(ids_ref[...], cfg.E)
    n = cfg.XC
    for k in range(cfg.NE):
        start = (idx_ref[1] ^ k) * n
        hot = hot_slots(slot_a, start, n) + hot_slots(slot_b, start, n)
        outs[k][...] = b16(dot(b16(hot), hidden, TN))


def arrange(cfg, cuts, order_ref, *refs):
    pieces, outs = refs[: cfg.NE], refs[cfg.NE :]
    rows = jnp.concatenate([p[...] for p in pieces], axis=0)
    total = rows.shape[0]
    part = total // HALVES
    for n in range(HALVES):
        hot = (iota((part, total), 0) + n * part == order_ref[...]).astype(jnp.float32)
        half = b16(dot(b16(hot), rows))
        for m, (lo, hi) in enumerate(cuts):
            outs[n * len(cuts) + m][...] = half[:, lo:hi]


def gather_sum(cfg, idx_ref, order_ref, *refs):
    ins, outs = refs[: HALVES * cfg.NC], refs[HALVES * cfg.NC :]
    halves = []
    for n in range(HALVES):
        group = ins[n * cfg.NC : (n + 1) * cfg.NC]
        total = f32(group[0][...])
        for piece in group[1:]:
            total = total + f32(piece[...])
        halves.append(b16(total))
    rows = jnp.concatenate(halves, axis=0)
    count = rows.shape[0]
    place = order_ref[0:1]
    if len(outs) == 1:
        place = order_ref[1:2] + (order_ref[2:3] ^ idx_ref[1]) * CAP
    hot = (iota((count, count), 0) == place).astype(jnp.float32)
    back = b16(dot(b16(hot), rows, TN))
    if len(outs) == 1:
        outs[0][...] = back
        return
    for k, out in enumerate(outs):
        out[...] = back[k * cfg.XC : (k + 1) * cfg.XC]


def collect(cfg, idx_ref, ids, pieces):
    slot_a, slot_b = slots_of(ids, cfg.E)
    total = None
    if len(pieces) == 1:
        hot = hot_slots(slot_a, 0, cfg.E * CAP) + hot_slots(slot_b, 0, cfg.E * CAP)
        return dot(b16(hot), pieces[0][...])
    for k, piece in enumerate(pieces):
        start = (idx_ref[1] ^ k) * cfg.XC
        hot = hot_slots(slot_a, start, cfg.XC) + hot_slots(slot_b, start, cfg.XC)
        term = dot(b16(hot), piece[...])
        total = term if total is None else total + term
    return total


def finish_forward(cfg, idx_ref, ids_ref, mixed_ref, *refs):
    refs[-1][...] = mixed_ref[...] + collect(cfg, idx_ref, ids_ref[...], refs[:-1])


def moe_back(cfg, idx_ref, ids_ref, mixed_ref, gain_ref, up_ref, *refs):
    pieces = refs[: cfg.NE]
    mix_ref, half_ref, gg_ref = refs[cfg.NE :]
    grad = collect(cfg, idx_ref, ids_ref[...], pieces)
    unit, inverse = rms(mixed_ref[...])
    gg_ref[...] = jnp.broadcast_to(jnp.sum(grad * unit, axis=0, keepdims=True), (8, cfg.D))
    scaled = grad * gain_ref[1:2, :]
    moved = inverse * (scaled - unit * jnp.mean(scaled * unit, axis=-1, keepdims=True))
    grad_mixed = f32(up_ref[...]) + moved
    mix_ref[...] = grad_mixed
    half_ref[...] = b16(grad_mixed)


def joined(refs):
    return jnp.concatenate([r[...] for r in refs], axis=0)


def join_parts(refs, parts):
    rows = [jnp.concatenate([r[...] for r in refs[n : n + parts]], axis=1) for n in range(0, len(refs), parts)]
    return jnp.concatenate(rows, axis=0)


def expert_kernel(cfg, first, parts, idx_ref, *refs):
    NC, D, E = cfg.NC, cfg.D, cfg.E
    rows_in, refs = refs[:NC], refs[NC:]
    ups_in, refs = refs[: parts * NC], refs[parts * NC :]
    win_ref, wout_ref, router_ref = refs[:3]
    outs = refs[3:]
    back, fwd = outs[:NC], outs[NC : 2 * NC]
    rows_out, up_out, act_out, pre_out, route_out = outs[2 * NC :]
    step = pl.program_id(0)
    own = idx_ref[1] * cfg.X + first + step
    rows = joined(rows_in)
    ups = join_parts(ups_in, parts)
    count = rows.shape[0]
    win, wout = win_ref[0], wout_ref[0]
    other = ups[:, D : D + 1].astype(jnp.float32).astype(jnp.int32)
    up = f32(ups[:, :D])
    lane = iota((count, E), 1)
    is_own = (lane == own).astype(jnp.float32)
    is_other = (lane == other).astype(jnp.float32)
    sign = is_own - is_other
    gap = jnp.sum(dot(rows, router_ref[...]) * sign, axis=1, keepdims=True)
    gate = jax.nn.sigmoid(gap)
    against = jax.nn.sigmoid(-gap)
    up_rows = b16(gate * up)
    preact = dot(rows, win)
    cdf = 0.5 * (1.0 + lax.erf(preact * INV_ROOT_TWO))
    slope = cdf + preact * jnp.exp(-0.5 * preact * preact) * INV_ROOT_TAU
    active = b16(preact * cdf)
    part = dot(active, wout)
    grad_pre = b16(dot(up_rows, wout, NT) * slope)
    weight = gate * against * jnp.sum(up * part, axis=1, keepdims=True)
    coef = weight * sign
    high = b16(coef)
    low = b16(coef - f32(high))
    route_ref = router_ref[...]
    both = jnp.concatenate([f32(high), f32(low)], axis=1).astype(jnp.bfloat16)
    wide = jnp.concatenate([f32(route_ref), f32(route_ref)], axis=1).astype(jnp.bfloat16)
    back_rows = dot(grad_pre, win, NT) + dot(both, wide, NT)
    route = dot(rows, both, TN)

    @pl.when(step == 0)
    def _():
        route_out[...] = route

    @pl.when(step > 0)
    def _():
        route_out[...] += route

    fwd_rows = b16(gate * part)
    back_rows = b16(back_rows)
    each = count // NC
    for c in range(NC):
        back[c][...] = back_rows[c * each : (c + 1) * each]
        fwd[c][...] = fwd_rows[c * each : (c + 1) * each]
    rows_out[0] = rows
    up_out[0] = up_rows
    act_out[0] = active
    pre_out[0] = grad_pre


def experts(cfg, half, cuts, idx, rows, ups, w_in, w_out, router):
    NC, D, FL = cfg.NC, cfg.D, w_in.shape[2]
    steps = cfg.X // HALVES
    first = half * steps
    each = cfg.NE * CAP
    count = NC * each
    fixed = lambda shape: pl.BlockSpec(shape, lambda s: (0,) * len(shape))
    row = lambda w: pl.BlockSpec((each, w), lambda s: (s, 0))
    per = lambda a, b: pl.BlockSpec((1, a, b), lambda s: (first + s, 0, 0))
    here = lambda a, b: pl.BlockSpec((1, a, b), lambda s: (s, 0, 0))
    saved = [((steps, count, w), jnp.bfloat16) for w in (D, D, FL, FL)]
    outs = [((steps * each, D), jnp.bfloat16)] * (2 * NC) + saved + [((D, 2 * cfg.E), jnp.float32)]
    in_specs = [SMEM] + [row(D)] * NC + [row(hi - lo) for lo, hi in cuts] * NC
    in_specs += [per(D, FL), per(FL, D), fixed((D, cfg.E))]
    out_specs = [row(D)] * (2 * NC) + [here(count, w) for w in (D, D, FL, FL)]
    out_specs += [fixed((D, 2 * cfg.E))]
    return pl.pallas_call(
        functools.partial(expert_kernel, cfg, first, len(cuts)),
        grid=(steps,),
        out_shape=[jax.ShapeDtypeStruct(s, d) for s, d in outs],
        in_specs=in_specs,
        out_specs=out_specs,
        cost_estimate=pl.CostEstimate(
            flops=steps * 4 * 2 * count * D * FL, bytes_accessed=steps * 4 * D * FL, transcendentals=0
        ),
    )(idx, *rows, *ups, w_in, w_out, router)


def expert_weights_kernel(rows_ref, up_ref, act_ref, pre_ref, *refs):
    gin_ref, gout_ref = refs[-2:]
    gin_ref[0] = dot(rows_ref[0], pre_ref[0], TN)
    gout_ref[0] = dot(act_ref[0], up_ref[0], TN)


def expert_weights(cfg, half, rows, up, act, pre, earlier):
    steps, count, D = rows.shape
    FL = act.shape[2]
    here = lambda a, b: pl.BlockSpec((1, a, b), lambda s: (s, 0, 0))
    per = lambda a, b: pl.BlockSpec((1, a, b), lambda s: (half * steps + s, 0, 0))
    return pl.pallas_call(
        expert_weights_kernel,
        grid=(steps,),
        out_shape=[
            jax.ShapeDtypeStruct((cfg.X, D, FL), jnp.float32),
            jax.ShapeDtypeStruct((cfg.X, FL, D), jnp.float32),
        ],
        in_specs=[here(count, D), here(count, D), here(count, FL), here(count, FL)]
        + [pl.BlockSpec(memory_space=pl.ANY)] * len(earlier),
        out_specs=[per(D, FL), per(FL, D)],
        input_output_aliases={4 + n: n for n in range(len(earlier))},
        cost_estimate=pl.CostEstimate(
            flops=steps * 4 * count * D * FL, bytes_accessed=steps * 8 * D * FL, transcendentals=0
        ),
    )(rows, up, act, pre, *earlier)


def attn_backward(
    cfg, idx_ref, x_ref, bucket_ref, wo_ref, q_ref, k_ref, v_ref, hid_ref, lse_ref,
    bias_ref, w_ref, gain_ref, gg_ref, *refs,
):
    NC = cfg.NC
    routes, refs = refs[:HALVES], refs[HALVES:]
    gm_in, atts, refs = refs[:NC], refs[NC : 2 * NC], refs[2 * NC :]
    mine_ref, part_ref, *gh_out = refs[: 2 + NC]
    da_ref, dq_ref, dk_ref, dv_ref, p_ref, ds_ref, acc_ref, dw_ref, gm_ref, gh_ref = refs[2 + NC :]
    D, S, hl, CQ, CO, B = cfg.D, cfg.S, cfg.hl, cfg.CQ, cfg.CO, cfg.B
    nb = S // TILE
    c = idx_ref[0]
    place_blocks(cfg, idx_ref, gm_in, gm_ref)
    gm = gm_ref[...]
    own = pl.multiple_of(c * CQ, CQ)
    grad_att = b16(dot(gm, wo_ref[pl.ds(own, CQ), :], NT))
    for h in range(hl):
        da_ref[h] = grad_att[:, h * HD : (h + 1) * HD]
    prod = f32(grad_att) * f32(atts[0][...])
    deltas = [jnp.sum(prod[:, h * HD : (h + 1) * HD], axis=1, keepdims=True) for h in range(hl)]
    acc_ref[...] = jnp.zeros_like(acc_ref)
    for ib in range(nb):
        if ib + 1 < nb:
            zero = jnp.zeros((TILE, S - (ib + 1) * TILE), jnp.bfloat16)
            p_ref[ib * TILE : (ib + 1) * TILE, (ib + 1) * TILE :] = zero
            ds_ref[ib * TILE : (ib + 1) * TILE, (ib + 1) * TILE :] = zero
    for h in range(hl):
        for ib in range(nb):
            lo, n = ib * TILE, (ib + 1) * TILE
            s = dot(q_ref[h, lo:n], k_ref[h, 0:n], NT)
            s = s + jnp.concatenate([bias_ref[h, ib - jb] for jb in range(ib + 1)], axis=1)
            prob = jnp.exp(s - lse_ref[h, lo:n])
            grad_p = dot(da_ref[h, lo:n], v_ref[h, 0:n], NT)
            grad_s = prob * (grad_p - deltas[h][lo:n])
            p_ref[lo:n, 0:n] = b16(prob)
            half = b16(grad_s)
            ds_ref[lo:n, 0:n] = half
            dq_ref[h, lo:n] = dot(half, k_ref[h, 0:n]) * SCALE
            for jb in range(ib + 1):
                acc_ref[h, ib - jb] += grad_s[:, jb * TILE : (jb + 1) * TILE]
        dk_ref[h] = dot(ds_ref[...], q_ref[h], TN)
        dv_ref[h] = dot(p_ref[...], da_ref[h], TN)
    per_offset = []
    zero_tile = jnp.zeros((TILE, TILE), jnp.float32)
    sub = iota((8, 2 * TILE), 0)
    for h in range(hl):
        rows = []
        for k in range(nb):
            wide = jnp.concatenate([jnp.transpose(acc_ref[h, k]), zero_tile], axis=1)
            total = wide[0:8]
            for g in range(1, TILE // 8):
                total = total + pltpu.roll(wide[g * 8 : (g + 1) * 8], 2 * TILE - 8 * g, 1)
            for bit in (1, 2, 4):
                total = jnp.where((sub & bit) != 0, pltpu.roll(total, 2 * TILE - bit, 1), total)
            rows.append(jnp.sum(total, axis=0, keepdims=True))
        spans = []
        for k in range(nb):
            span = rows[k][:, :TILE]
            if k + 1 < nb:
                span = span + rows[k + 1][:, TILE:]
            spans.append(span)
        per_offset.append(jnp.concatenate(spans, axis=1))
    per_offset.append(jnp.zeros((8 - hl, S), jnp.float32))
    per_offset = jnp.concatenate(per_offset, axis=0)
    hot = (iota((cfg.NB, S), 0) == bucket_ref[...]).astype(jnp.float32)
    table = dot(per_offset, hot, NT, lax.Precision.HIGHEST)
    place = table_select(cfg.NB, D, cfg.rows, cfg.NE).astype(jnp.float32)
    table_rows = dot(table, place, NN, lax.Precision.HIGHEST)
    grads = jnp.concatenate(
        [dq_ref[h] for h in range(hl)] + [dk_ref[h] for h in range(hl)] + [dv_ref[h] for h in range(hl)],
        axis=1,
    )
    grads = b16(grads)
    dw_ref[0:D, : 3 * CQ] = dot(hid_ref[...], grads, TN)
    sel = b16((iota((D, CO), 0) == c * CO + iota((D, CO), 1)).astype(jnp.float32))
    gm_cols = b16(dot(gm, sel))
    for k in range(NC):
        heads = pl.multiple_of((c ^ k) * CQ, CQ)
        dw_ref[pl.ds(heads, CQ), 3 * CQ : 3 * CQ + CO] = dot(atts[k][...], gm_cols, TN)
    gh = dot(grads, w_ref[:, : 3 * CQ], NT)
    gh_ref[...] = b16(gh)
    for k, out in enumerate(gh_out):
        out[...] = gh_ref[pl.ds(pl.multiple_of((c ^ k) * B, B), B), :]
    unit, _ = rms(f32(x_ref[...]))
    gain_one = jnp.sum(gh * unit, axis=0, keepdims=True)
    E = cfg.E
    stack = jnp.concatenate(
        [
            jnp.zeros((E, D), jnp.float32),
            gain_one,
            gg_ref[0:1, :],
            table_rows[0:hl],
            jnp.zeros((EXTRA - E - 2 - hl, D), jnp.float32),
        ],
        axis=0,
    )
    extra = jnp.transpose(stack)
    route = routes[0][...]
    for r in routes[1:]:
        route = route + r[...]
    route = route[:, :E] + route[:, E:]
    extra = extra + jnp.concatenate([route, jnp.zeros((D, EXTRA - E), jnp.float32)], axis=1)
    dw_ref[0:D, 3 * CQ + CO :] = extra
    me = idx_ref[1]
    R = cfg.rows
    for j in range(cfg.NE // 2):
        a = pl.multiple_of((me ^ (2 * j)) * R, R)
        b = pl.multiple_of((me ^ (2 * j + 1)) * R, R)
        mine_ref[j * R : (j + 1) * R, :] = b16(dw_ref[pl.ds(a, R), :])
        part_ref[j * R : (j + 1) * R, :] = b16(dw_ref[pl.ds(b, R), :])


def add_pairs(cfg, a_ref, b_ref, *outs):
    R = cfg.rows
    for j, out in enumerate(outs):
        out[...] = b16(f32(a_ref[j * R : (j + 1) * R]) + f32(b_ref[j * R : (j + 1) * R]))


def add_all(*refs):
    total = f32(refs[0][...])
    for r in refs[1:-1]:
        total = total + f32(r[...])
    refs[-1][...] = b16(total)


def last_input(x_ref, gain_ref, mix_ref, *refs):
    out_ref = refs[-1]
    total = f32(refs[0][...])
    for ref in refs[1:-1]:
        total = total + f32(ref[...])
    unit, inverse = rms(f32(x_ref[...]))
    scaled = total * gain_ref[0:1, :]
    moved = inverse * (scaled - unit * jnp.mean(scaled * unit, axis=-1, keepdims=True))
    out_ref[...] = mix_ref[...] + moved


def last_weights(cfg, idx_ref, *refs):
    ins, (q_ref, k_ref, v_ref, o_ref, router_ref, one_ref, two_ref, table_ref, all_ref) = refs[: cfg.NC], refs[cfg.NC :]
    R, CQ, CO, D, hl, E = cfg.rows, cfg.CQ, cfg.CO, cfg.D, cfg.hl, cfg.E
    for k, piece in enumerate(ins):
        all_ref[idx_ref[0] ^ k] = f32(piece[...])
    pieces = [all_ref[n] for n in range(cfg.NC)]
    for t, ref in enumerate((q_ref, k_ref, v_ref)):
        full = jnp.concatenate([p[:, t * CQ : (t + 1) * CQ] for p in pieces], axis=1)
        ref[...] = full[:, :D]
    o_ref[...] = jnp.concatenate([p[:, 3 * CQ : 3 * CQ + CO] for p in pieces], axis=1)
    base = 3 * CQ + CO
    extra = pieces[0][:, base:]
    for p in pieces[1:]:
        extra = extra + p[:, base:]
    router_ref[...] = jnp.transpose(extra)[:E]
    eye = (iota((R, R), 0) == iota((R, R), 1)).astype(jnp.float32)
    one_ref[...] = jnp.sum(eye * extra[:, E : E + 1], axis=0, keepdims=True)
    two_ref[...] = jnp.sum(eye * extra[:, E + 1 : E + 2], axis=0, keepdims=True)
    table = jnp.concatenate([p[:, base + E + 2 : base + E + 2 + hl] for p in pieces], axis=1)
    table_ref[...] = table[: cfg.NB // cfg.NE, : cfg.H]


class Config:
    def pair(self, pieces):
        if len(pieces) == 1:
            return list(pieces)
        return list(zip(self.orders, pieces, strict=True))


def permute(x, axis, k, n):
    return lax.ppermute(x, axis, [(i, i ^ k) for i in range(n)])


def spread(first, rest, axis, n):
    return [first] + [permute(x, axis, k, n) for k, x in zip(range(1, n), rest, strict=True)]


def spread_far_first(first, rest, n):
    got = [first] + [None] * (n - 1)
    for ks in (range(n // 2, n), range(1, n // 2)):
        for k in ks:
            got[k] = permute(rest[k - 1], "ep", k, n)
    return got


def two_steps(parts):
    got = []
    for part, (near, via) in zip(parts, ((1, 2), (2, 1)), strict=True):
        one, two = permute(part, "ctx", near, 4), permute(part, "ctx", via, 4)
        far = permute(one, "ctx", via, 4)
        got.append([part, one, two, far] if near == 1 else [part, two, one, far])
    return got


def gather_rows(cfg, x):
    if len(cfg.orders) == 1:
        return [lax.all_gather(x, "ep", axis=0, tiled=True)]
    got = [x] + [permute(x, "ep", 2 * j, cfg.NE) for j in range(1, cfg.NE // 2)]
    return got + [permute(g, "ep", 1, cfg.NE) for g in got]


def body(
    block_input, out_grad, w_query, w_key, w_value, w_output, w_router, attn_gain, moe_gain,
    bias_table, rel_bucket, expert_ids, expert_in, expert_out,
):
    cfg = Config()
    NC, NE = lax.axis_size("ctx"), lax.axis_size("ep")
    B, D = block_input.shape[1:]
    S = rel_bucket.shape[0]
    cfg.NC, cfg.NE, cfg.B, cfg.D, cfg.S = NC, NE, B, D, S
    cfg.H = D // HD
    cfg.hl = -(-cfg.H // NC)
    cfg.CQ = CQ = cfg.hl * HD
    cfg.CO = CO = D // NC
    cfg.rows = R = D // NE
    cfg.X = X = expert_in.shape[0]
    cfg.E = E = X * NE
    cfg.XC = X * CAP
    cfg.NB = bias_table.shape[0] * NE
    hl = cfg.hl
    if R % 16 == 0:
        cfg.orders = [(2 * j,) for j in range(NE // 2)] + [(2 * j + 1,) for j in range(NE // 2)]
    else:
        cfg.orders = [None]
    bf, fl = jnp.bfloat16, jnp.float32
    c, e = lax.axis_index("ctx"), lax.axis_index("ep")
    idx = jnp.stack([c, e]).astype(jnp.int32)
    x_own, up_own, ids = block_input[0], out_grad[0], expert_ids[0]
    bucket = rel_bucket.reshape(1, S)

    W1 = 3 * CQ + HD
    pack_a, pack_b = call(
        functools.partial(pack_weights, cfg),
        [idx, w_query, w_key, w_value, w_output, w_router.T, attn_gain[None], moe_gain[None], bias_table],
        [((R, W1), bf), ((R, D + E), bf)], scratch=[pltpu.VMEM((R, TILE), fl)],
    )
    first = gather_rows(cfg, pack_a)
    x_pieces = spread(x_own, [x_own] * (NC - 1), "ctx", NC)
    second = gather_rows(cfg, pack_b)
    up_send = call(functools.partial(send_upstream, cfg), [idx, ids, up_own], [((cfg.XC, D + EXTRA), bf)] * NE)
    ks = np.arange(E * CAP)
    to = (ks % cfg.XC) // CAP * (NE * CAP) + ks // cfg.XC * CAP + ks % CAP
    order = jnp.asarray(to.reshape(1, -1), jnp.int32)
    source = ks // cfg.XC
    orders = jnp.asarray(np.stack([to, to - source * CAP, source]), jnp.int32)

    def to_experts(sent, cuts):
        got = spread_far_first(sent[0], sent[1:], NE)
        parts = call(
            functools.partial(arrange, cfg, cuts), [order, *got],
            [((E * CAP // HALVES, hi - lo), bf) for lo, hi in cuts] * HALVES, n_smem=0,
        )
        out = []
        for n in range(HALVES):
            here = parts[n * len(cuts) : (n + 1) * len(cuts)]
            if len(cuts) == 2 and NC == 4:
                got = two_steps(here)
            else:
                got = [spread(h, [h] * (NC - 1), "ctx", NC) for h in here]
            out.append([piece[k] for k in range(NC) for piece in got])
        return out

    def from_experts(parts, whole):
        got = []
        for half in parts:
            got += spread(half[0], half[1:], "ctx", NC)
        sent = call(
            functools.partial(gather_sum, cfg), [idx, orders, *got],
            [((E * CAP, D), bf)] if whole else [((cfg.XC, D), bf)] * NE,
        )
        if whole:
            return [lax.all_to_all(sent[0], "ep", split_axis=0, concat_axis=0, tiled=True)]
        return spread_far_first(sent[0], sent[1:], NE)

    W2 = D + EXTRA
    cut = (D // 2 + EXTRA - 1) // EXTRA * EXTRA
    cuts = ((0, cut), (cut, W2))
    ups = to_experts(up_send, cuts)
    nb = S // TILE
    x_all, q, k, v, hidden, att, lse, bias, w_all, gains = call(
        functools.partial(attn_forward, cfg), [idx, bucket, *first, *x_pieces],
        [((S, D), bf)] + [((hl, S, HD), bf)] * 3 + [((S, D), bf), ((S, CQ), bf), ((hl, S, 1), fl), ((hl, nb, TILE, TILE), fl),
         ((D, W1), bf), ((8, D), fl)],
        scratch=[pltpu.VMEM((hl, S, HD), fl)], flops=2e9,
    )
    atts = spread(att, [att] * (NC - 1), "ctx", NC)
    mixed, wo, router, *sent = call(
        functools.partial(middle, cfg), [idx, x_own, ids, gains, *atts, *second],
        [((B, D), fl), ((NC * CQ, D), bf), ((D, E), bf)] + [((cfg.XC, D), bf)] * NE,
        scratch=[pltpu.VMEM((D, D + E), bf)],
    )
    rows = to_experts(sent, ((0, D),))
    backs, fwds, routes, grads = [], [], [], []
    for half in range(HALVES):
        got = experts(cfg, half, cuts, idx, rows[half], ups[half], expert_in, expert_out, router)
        backs.append(got[:NC])
        fwds.append(got[NC : 2 * NC])
        grads = expert_weights(cfg, half, *got[2 * NC : 2 * NC + 4], grads)
        routes.append(got[-1])
    grad_expert_in, grad_expert_out = grads
    back = from_experts(backs, False)
    mix, mix_half, gg = call(
        functools.partial(moe_back, cfg), [idx, ids, mixed, gains, up_own, *back],
        [((B, D), fl), ((B, D), bf), ((8, D), fl)],
    )
    fwd = from_experts(fwds, True)
    (block_output,) = call(functools.partial(finish_forward, cfg), [idx, ids, mixed, *fwd], [((B, D), fl)])
    gm = spread(mix_half, [mix_half] * (NC - 1), "ctx", NC)
    WC = 3 * CQ + CO + EXTRA
    mine, part, *gh = call(
        functools.partial(attn_backward, cfg),
        [idx, x_all, bucket, wo, q, k, v, hidden, lse, bias, w_all, gains, gg, *routes, *gm, *atts],
        [((D // 2, WC), bf)] * 2 + [((B, D), bf)] * NC,
        scratch=[
            pltpu.VMEM((hl, S, HD), bf),
            pltpu.VMEM((hl, S, HD), fl),
            pltpu.VMEM((hl, S, HD), fl),
            pltpu.VMEM((hl, S, HD), fl),
            pltpu.VMEM((S, S), bf),
            pltpu.VMEM((S, S), bf),
            pltpu.VMEM((hl, nb, TILE, TILE), fl),
            pltpu.VMEM((NC * CQ, WC), fl),
            pltpu.VMEM((S, D), bf),
            pltpu.VMEM((S, D), bf),
        ],
        flops=4e9,
    )
    theirs = permute(part, "ep", 1, NE)
    gh = spread(gh[0], gh[1:], "ctx", NC)
    pairs = call(functools.partial(add_pairs, cfg), [mine, theirs], [((R, WC), bf)] * (NE // 2), n_smem=0)
    pairs = [pairs[0]] + [permute(pairs[j], "ep", 2 * j, NE) for j in range(1, NE // 2)]
    (total,) = call(add_all, pairs, [((R, WC), bf)], n_smem=0)
    everyone = spread(total, [total] * (NC - 1), "ctx", NC)
    (input_grad,) = call(last_input, [x_own, gains, mix, *gh], [((B, D), fl)], n_smem=0)
    nbl = bias_table.shape[0]
    gq, gk, gv, go, grouter, gone, gtwo, gtable = call(
        functools.partial(last_weights, cfg), [idx, *everyone],
        [((R, D), fl)] * 4 + [((E, R), fl), ((1, R), fl), ((1, R), fl), ((nbl, cfg.H), fl)],
        scratch=[pltpu.VMEM((NC, R, WC), fl)],
    )
    return (
        block_output[None], input_grad[None], gq, gk, gv, go, grouter.T, gone[0], gtwo[0], gtable,
        grad_expert_in, grad_expert_out,
    )


def solution(mesh):
    two, three = P("ep", None), P("ep", "ctx", None)
    in_specs = (three, three, two, two, two, two, two, P("ep"), P("ep"), two, P(), three, P("ep", None, "ctx"), three)
    out_specs = (three, three, two, two, two, two, two, P("ep"), P("ep"), two, P("ep", None, "ctx"), three)
    return jax.shard_map(body, mesh=mesh, in_specs=in_specs, out_specs=out_specs, check_vma=False)
```
